32 devices in a mesh: seq: 8 (over z, y), chan: 4 (over x, core).
Axes of the slice: x: 2, y: 2, z: 4, core: 2. Of those that a mesh axis runs over, the one named last changes fastest.
Arguments:
- proj_in: bfloat16 [3, 1024, 4096], P(None, 'seq', 'chan'), may hold values from -6 to 6
- taps: float32 [3, 3, 4096], P(None, None, 'chan'), may hold values from -3 to 3
- long_filter: float32 [1024, 256], P('seq'), may hold values from -6 to 6
- out_grad: bfloat16 [1024, 4096], P('seq', 'chan'), may hold values from -0.1875 to 0.1875
Outputs:
- input_grad: bfloat16 [3, 1024, 4096], P(None, 'seq', 'chan')
- long_grad: float32 [1024, 256], P('seq', 'chan')
- tap_grad: float32 [3, 3, 4096], P(None, None, 'chan')
The draws below stay inside these ranges and needn't reach their ends.
All inputs are finite; a program needn't handle non-finite values.
Results may differ from the reference program's by a relative error of at most 0.001.
Values may be sent and summed in bfloat16 or wider, within the bound.
A program may use at most 64 MiB of HBM per device.

```python
import math
import jax
import jax.numpy as jnp
from jax import lax

D = 4096
G = 256
K = 3
TOKENS = 1024


def steps_of(own_key, extent, split, smallest, top_value):
    loudness = 1.0
    for position, blocks in split:
        draws = jax.random.uniform(jax.random.fold_in(jax.random.fold_in(own_key, 6), position), (blocks,), jnp.float32, smallest / len(split), top_value / len(split))
        loudness = loudness * jnp.repeat(jnp.exp(draws), extent[position] // blocks).reshape((-1,) + (1,) * (len(extent) - 1 - position))
    return loudness


def bell_draw(rng, extent, width, bound, cuts=(), held_as=jnp.bfloat16):
    entries = jax.random.normal(rng, extent, jnp.float32) * width
    if len(cuts) > 0:
        entries = steps_of(rng, extent, cuts, -0.22, 0.18) * entries
    return jnp.clip(entries, min=-bound, max=bound).astype(held_as)


def setup_inputs(seed: int = 0) -> dict:
    splits = jax.random.split(jax.random.key(seed), 5)
    proj_in = bell_draw(splits[0], (3, TOKENS, D), 1.0, 6.0, ((1, 8), (2, 4)))
    taps = bell_draw(splits[1], (3, K, D), 0.6, 3.0, ((2, 4),), jnp.float32)
    long_filter = bell_draw(splits[2], (TOKENS, G), 1.0, 6.0, ((0, 8),), jnp.float32)
    out_grad = bell_draw(splits[3], (TOKENS, D), TOKENS ** -0.5, 0.1875, ((0, 8), (1, 4)))
    return {"proj_in": proj_in, "taps": taps, "long_filter": long_filter, "out_grad": out_grad}


def delayed(values, lag_step):
    if lag_step == 0:
        return values
    padding = jnp.zeros((values.shape[0], lag_step, values.shape[2]), values.dtype)
    return jnp.concatenate([padding, values[:, :values.shape[1] - lag_step]], axis=1)

def advanced(values, lag_step):
    if lag_step == 0:
        return values
    padding = jnp.zeros((values.shape[0], lag_step, values.shape[2]), values.dtype)
    return jnp.concatenate([values[:, lag_step:], padding], axis=1)

def reference(proj_in, taps, long_filter, out_grad):
    inputs = proj_in.astype(jnp.float32)
    lagged = [delayed(inputs, lag_step) for lag_step in range(K)]
    featured = taps[:, 0, None, :] * lagged[0]
    for lag_step in range(1, K):
        featured = featured + taps[:, lag_step, None, :] * lagged[lag_step]
    query_rows, key_rows, value_rows = (featured[0], featured[1], featured[2])
    mixed_rows = key_rows * value_rows
    upstream = out_grad.astype(jnp.float32)
    conv_grad = upstream * query_rows
    length = 2 * TOKENS
    blocks = D // G
    filt_spec = jnp.fft.rfft(long_filter, n=length, axis=0)
    mixed_blocks = mixed_rows.reshape(TOKENS, blocks, G).transpose(1, 0, 2)
    grad_blocks = conv_grad.reshape(TOKENS, blocks, G).transpose(1, 0, 2)

    def one_block(pair):
        mixed_part, grad_part = pair
        mix_spec = jnp.fft.rfft(mixed_part, n=length, axis=0)
        grad_spec = jnp.fft.rfft(grad_part, n=length, axis=0)
        conv_part = jnp.fft.irfft(filt_spec * mix_spec, n=length, axis=0)[:TOKENS]
        back_part = jnp.fft.irfft(jnp.conj(filt_spec) * grad_spec, n=length, axis=0)[:TOKENS]
        corr_part = jnp.fft.irfft(grad_spec * jnp.conj(mix_spec), n=length, axis=0)[:TOKENS]
        return (conv_part, back_part, corr_part)
    conv_blocks, back_blocks, corr_blocks = lax.map(one_block, (mixed_blocks, grad_blocks))
    conv_out = conv_blocks.transpose(1, 0, 2).reshape(TOKENS, D)
    mixed_grad = back_blocks.transpose(1, 0, 2).reshape(TOKENS, D)
    long_grad = lax.optimization_barrier(jnp.sum(corr_blocks, axis=0))
    feature_grad = jnp.stack([upstream * conv_out, mixed_grad * value_rows, mixed_grad * key_rows], axis=0)
    input_grad = taps[:, 0, None, :] * feature_grad
    for lag_step in range(1, K):
        input_grad = input_grad + taps[:, lag_step, None, :] * advanced(feature_grad, lag_step)
    tap_grad = jnp.stack([lax.optimization_barrier(jnp.sum(feature_grad * lagged[lag_step], axis=1)) for lag_step in range(K)], axis=1)
    tap_grad = tap_grad / math.sqrt(TOKENS)
    return (input_grad.astype(jnp.bfloat16), long_grad, tap_grad)
```

```python
import functools
import math

import jax
import jax.numpy as jnp
import numpy as np
from jax import lax
from jax.experimental import pallas as pl
from jax.experimental.pallas import tpu as pltpu
from jax.sharding import PartitionSpec as P

MESH = pl.DeviceIdType.MESH
LANES = 128
TABLE_LIMIT = 1024


def shifted(x, axis, by):
    devices = lax.axis_size(axis)
    pairs = [(i, i + by) for i in range(devices) if 0 <= i + by < devices]
    return lax.ppermute(x, axis, pairs)


def angle_table(left_index, right_index, period):
    product = left_index[:, None] * right_index[None, :] % period
    phase = product.astype(jnp.float32) * (2.0 * math.pi / period)
    return (jnp.cos(phase), jnp.sin(phase))


def contract(pattern, factor_table, operand):
    return jnp.einsum(pattern, factor_table, operand, precision=lax.Precision.HIGHEST)


def steps_of(count):
    return jnp.arange(count, dtype=jnp.int32)


def whole_forward(signal, seq_width):
    tok_rows, stack_count, channels = signal.shape
    period = 2 * seq_width * tok_rows
    narrow = channels // seq_width
    arrived = lax.all_to_all(signal, "seq", split_axis=2, concat_axis=0, tiled=True)
    laid = arrived.reshape(seq_width, tok_rows, stack_count, narrow).transpose(2, 3, 0, 1)
    cos_step, sin_step = angle_table(steps_of(2 * seq_width), steps_of(seq_width), 2 * seq_width)
    real_part = contract("qm,ncmj->ncqj", cos_step, laid)
    imag_part = -contract("qm,ncmj->ncqj", sin_step, laid)
    cos_turn, sin_turn = angle_table(steps_of(2 * seq_width), steps_of(tok_rows), period)
    turned_re = real_part * cos_turn + imag_part * sin_turn
    turned_im = imag_part * cos_turn - real_part * sin_turn
    cos_row, sin_row = angle_table(steps_of(tok_rows), steps_of(tok_rows), tok_rows)
    spec_re = contract("rj,ncqj->ncqr", cos_row, turned_re) + contract(
        "rj,ncqj->ncqr", sin_row, turned_im
    )
    spec_im = contract("rj,ncqj->ncqr", cos_row, turned_im) - contract(
        "rj,ncqj->ncqr", sin_row, turned_re
    )
    return (spec_re, spec_im)


def whole_inverse(spec_re, spec_im, seq_width):
    stack_count, narrow, freq_count, tok_rows = spec_re.shape
    period = 2 * seq_width * tok_rows
    cos_row, sin_row = angle_table(steps_of(tok_rows), steps_of(tok_rows), tok_rows)
    back_re = contract("rj,ncqr->ncqj", cos_row, spec_re) - contract(
        "rj,ncqr->ncqj", sin_row, spec_im
    )
    back_im = contract("rj,ncqr->ncqj", sin_row, spec_re) + contract(
        "rj,ncqr->ncqj", cos_row, spec_im
    )
    cos_turn, sin_turn = angle_table(steps_of(freq_count), steps_of(tok_rows), period)
    turned_re = back_re * cos_turn - back_im * sin_turn
    turned_im = back_re * sin_turn + back_im * cos_turn
    cos_step, sin_step = angle_table(steps_of(seq_width), steps_of(freq_count), freq_count)
    signal = contract("mq,ncqj->ncmj", cos_step, turned_re) - contract(
        "mq,ncqj->ncmj", sin_step, turned_im
    )
    signal = (
        (signal / period).transpose(2, 3, 0, 1).reshape(seq_width * tok_rows, stack_count, narrow)
    )
    return lax.all_to_all(signal, "seq", split_axis=0, concat_axis=2, tiled=True)


def member(values, index, stack_axis):
    return lax.index_in_dim(values, index, stack_axis, keepdims=False)


def shards(proj_in, taps, long_filter, out_grad):
    stream_count, tok_rows, channels = proj_in.shape
    tap_count = taps.shape[1]
    groups = long_filter.shape[1]
    seq_width = lax.axis_size("seq")
    lower_rim = shifted(proj_in[:, tok_rows - (tap_count - 1) :, :], "seq", 1)
    extended = jnp.concatenate([lower_rim, proj_in], axis=1).astype(jnp.float32)
    lagged = [
        extended[:, tap_count - 1 - lag_step : tap_count - 1 - lag_step + tok_rows, :]
        for lag_step in range(tap_count)
    ]
    featured = taps[:, 0, None, :] * lagged[0]
    for lag_step in range(1, tap_count):
        featured = featured + taps[:, lag_step, None, :] * lagged[lag_step]
    query_rows, key_rows, value_rows = (featured[0], featured[1], featured[2])
    mixed_rows = key_rows * value_rows
    upstream = out_grad.astype(jnp.float32)
    conv_grad = upstream * query_rows
    tiled_filter = jnp.tile(long_filter, (1, channels // groups))
    signals = jnp.stack([mixed_rows, conv_grad, tiled_filter], axis=1)
    data_re, data_im = whole_forward(signals, seq_width)
    stack_axis = 0
    mix_re, mix_im = (member(data_re, 0, stack_axis), member(data_im, 0, stack_axis))
    grad_re, grad_im = (member(data_re, 1, stack_axis), member(data_im, 1, stack_axis))
    filt_re, filt_im = (member(data_re, 2, stack_axis), member(data_im, 2, stack_axis))
    conv_re = filt_re * mix_re - filt_im * mix_im
    conv_im = filt_re * mix_im + filt_im * mix_re
    back_re = filt_re * grad_re + filt_im * grad_im
    back_im = filt_re * grad_im - filt_im * grad_re
    corr_re = grad_re * mix_re + grad_im * mix_im
    corr_im = grad_im * mix_re - grad_re * mix_im
    prod_re = jnp.stack([conv_re, back_re, corr_re], axis=stack_axis)
    prod_im = jnp.stack([conv_im, back_im, corr_im], axis=stack_axis)
    outputs = whole_inverse(prod_re, prod_im, seq_width)
    conv_out, mixed_grad = (outputs[:, 0], outputs[:, 1])
    filt_grad = jnp.sum(outputs[:, 2].reshape(tok_rows, channels // groups, groups), axis=1)
    long_grad = lax.psum_scatter(filt_grad, "chan", scatter_dimension=1, tiled=True)
    feature_grad = jnp.stack(
        [upstream * conv_out, mixed_grad * value_rows, mixed_grad * key_rows], axis=0
    )
    upper_rim = shifted(feature_grad[:, : tap_count - 1, :], "seq", -1)
    trailing = jnp.concatenate([feature_grad, upper_rim], axis=1)
    input_grad = taps[:, 0, None, :] * feature_grad
    for lag_step in range(1, tap_count):
        input_grad = (
            input_grad + taps[:, lag_step, None, :] * trailing[:, lag_step : lag_step + tok_rows]
        )
    partial_taps = jnp.stack(
        [jnp.sum(feature_grad * lagged[lag_step], axis=1) for lag_step in range(tap_count)], axis=1
    )
    tap_grad = lax.psum(partial_taps, "seq") / math.sqrt(seq_width * tok_rows)
    return (input_grad.astype(jnp.bfloat16), long_grad, tap_grad)


def meet(axis_sizes):
    barrier = pltpu.get_barrier_semaphore()
    total = 0
    for axis, size in axis_sizes:
        me = lax.axis_index(axis)
        for j in range(1, size):
            pl.semaphore_signal(
                barrier, inc=1, device_id={axis: lax.rem(me + j, size)}, device_id_type=MESH
            )
        total += size - 1
    pl.semaphore_wait(barrier, total)


def swap_matrix(reps, width):
    side = reps * LANES
    row = lax.broadcasted_iota(jnp.int32, (side, side), 0)
    col = lax.broadcasted_iota(jnp.int32, (side, side), 1)
    outer, inner, rest = row // LANES, (row % LANES) // width, row % width
    hit = inner * LANES + outer * width + rest == col
    return jnp.where(hit, 1.0, 0.0).astype(jnp.bfloat16)


def lane_group(rows, width):
    return lax.broadcasted_iota(jnp.int32, (rows, LANES), 1) // width


def turn(x, shift, axis):
    shift = shift % x.shape[axis]
    return x if shift == 0 else pltpu.roll(x, shift, axis)


def spread_kernel(n, reps, x_ref, og_ref, lf_ref, rb_ref, fr_ref, sb, fs, dsend, drecv, fsend, frecv):
    me = lax.axis_index("seq")
    width = LANES // reps
    streams, rows, _ = x_ref.shape
    meet([("seq", n)])
    part = rows // reps
    grp = lane_group(part, width)
    for s in range(n):
        base = (s // reps) * LANES
        packed = jnp.zeros((part, LANES), jnp.float32)
        for q in range(reps):
            tile = lf_ref[q * part : (q + 1) * part, base : base + LANES]
            packed = jnp.where(grp == q, turn(tile, (q - s % reps) * width, 1), packed)
        fs[s] = packed
    copies = []
    for j in range(1, n):
        peer = lax.rem(me + j, n)
        copy = pltpu.make_async_remote_copy(
            src_ref=fs.at[peer], dst_ref=fr_ref.at[me], send_sem=fsend.at[j - 1],
            recv_sem=frecv.at[j - 1], device_id={"seq": peer}, device_id_type=MESH,
        )
        copy.start()
        copies.append(copy)
    swap = swap_matrix(reps, width)
    tiles = n // reps
    for h in range(tiles):
        for p in range(streams + 1):
            source = x_ref.at[p] if p < streams else og_ref
            joined = jnp.concatenate(
                [source[:, (r * tiles + h) * LANES : (r * tiles + h + 1) * LANES] for r in range(reps)],
                axis=1,
            )
            moved = jnp.dot(joined, swap, preferred_element_type=jnp.float32).astype(jnp.bfloat16)
            for g in range(reps):
                sb[h * reps + g, p] = moved[:, g * LANES : (g + 1) * LANES]
    for j in range(1, n):
        peer = lax.rem(me + j, n)
        copy = pltpu.make_async_remote_copy(
            src_ref=sb.at[peer], dst_ref=rb_ref.at[me], send_sem=dsend.at[j - 1],
            recv_sem=drecv.at[j - 1], device_id={"seq": peer}, device_id_type=MESH,
        )
        copy.start()
        copies.append(copy)
    rb_ref[me] = sb[me]
    fr_ref[me] = fs[me]
    for copy in copies:
        copy.wait()


def halves(x):
    high = x.astype(jnp.bfloat16)
    return high, (x - high.astype(jnp.float32)).astype(jnp.bfloat16)


def later(x, lag):
    if lag == 0:
        return x
    row = lax.broadcasted_iota(jnp.int32, x.shape, 0)
    return jnp.where(row < lag, 0.0, pltpu.roll(x, lag, 0))


def sooner(x, lag):
    if lag == 0:
        return x
    row = lax.broadcasted_iota(jnp.int32, x.shape, 0)
    return jnp.where(row >= x.shape[0] - lag, 0.0, pltpu.roll(x, x.shape[0] - lag, 0))


def group_sum(x, reps):
    total = x
    for r in range(1, reps):
        total = total + turn(x, r * (LANES // reps), 1)
    return total


def three(high, low, x_high, x_low):
    def dot(a, b):
        return jnp.dot(a, b, preferred_element_type=jnp.float32)

    return dot(high, x_high) + (dot(high, x_low) + dot(low, x_high))


def make_table(ca, sa, cb, sb, ch, cl, sh, sl):
    step = cb.shape[0]

    @pl.loop(0, ca.shape[0])
    def _(i):
        c0, s0 = ca[pl.ds(i, 1), :], sa[pl.ds(i, 1), :]
        rows = pl.ds(pl.multiple_of(i * step, step), step)
        ch[rows, :], cl[rows, :] = halves(c0 * cb[...] - s0 * sb[...])
        sh[rows, :], sl[rows, :] = halves(s0 * cb[...] + c0 * sb[...])


def layer_kernel(
    n, reps, rb_ref, fr_ref, tp_ref, ca, sa, cb, sb, ig_ref, lg_ref, tg_ref,
    ch, cl, sh, sl, xh, xl, ah, al, bh, bl, res,
):
    me = lax.axis_index("seq")
    rows = rb_ref.shape[2]
    tokens = n * rows
    width = LANES // reps
    part = rows // reps
    taps = tp_ref[me]
    tap_count = 3
    make_table(ca, sa, cb, sb, ch, cl, sh, sl)

    def stream(p):
        return rb_ref[:, p].reshape(tokens, LANES).astype(jnp.float32)

    def feature(p):
        x = stream(p)
        total = taps[tap_count * p][None, :] * x
        for lag in range(1, tap_count):
            total = total + taps[tap_count * p + lag][None, :] * later(x, lag)
        return total

    def alternating(count):
        row = lax.broadcasted_iota(jnp.int32, (count, LANES), 0)
        return jnp.where(row % 2 == 0, 1.0, -1.0)

    sign = alternating(tokens)
    mixed = feature(1) * feature(2)
    xh[:, :LANES], xl[:, :LANES] = halves(mixed)
    mixed_end = jnp.sum(sign * mixed, axis=0, keepdims=True)
    grad = stream(3) * feature(0)
    xh[:, LANES : 2 * LANES], xl[:, LANES : 2 * LANES] = halves(grad)
    grad_end = jnp.sum(sign * grad, axis=0, keepdims=True)
    grp = lane_group(part, width)
    filt_end = jnp.zeros((1, LANES), jnp.float32)
    for s in range(n):
        packed = fr_ref[s]
        for q in range(reps):
            piece = group_sum(jnp.where(grp == q, packed, 0.0), reps)
            filt_end = filt_end + jnp.sum(alternating(part) * piece, axis=0, keepdims=True)
            at = s * rows + q * part
            xh[at : at + part, 2 * LANES :], xl[at : at + part, 2 * LANES :] = halves(piece)
    chunk = min(256, tokens)

    @pl.loop(0, tokens // chunk)
    def _(i):
        at = pl.ds(pl.multiple_of(i * chunk, chunk), chunk)
        a = three(ch[at, :], cl[at, :], xh[...], xl[...])
        b = three(sh[at, :], sl[at, :], xh[...], xl[...])
        am, ag, af = (a[:, k * LANES : (k + 1) * LANES] for k in range(3))
        bm, bg, bf = (b[:, k * LANES : (k + 1) * LANES] for k in range(3))
        row = lax.broadcasted_iota(jnp.int32, (chunk, LANES), 0) + i * chunk
        weight = jnp.where(row == 0, 0.5 / tokens, 1.0 / tokens)
        evens = (af * am - bf * bm, af * ag + bf * bg, group_sum(ag * am + bg * bm, reps))
        odds = (af * bm + bf * am, af * bg - bf * ag, group_sum(bg * am - ag * bm, reps))
        for k in range(3):
            lanes = slice(k * LANES, (k + 1) * LANES)
            ah[at, lanes], al[at, lanes] = halves(evens[k] * weight)
            bh[at, lanes], bl[at, lanes] = halves(odds[k] * weight)

    ends = jnp.concatenate(
        [filt_end * mixed_end, filt_end * grad_end, group_sum(grad_end * mixed_end, reps)], axis=1
    ) * (0.5 / tokens)

    @pl.loop(0, tokens // chunk)
    def _(i):
        at = pl.ds(pl.multiple_of(i * chunk, chunk), chunk)
        total = three(ch[at, :], cl[at, :], ah[...], al[...])
        total = total + three(sh[at, :], sl[at, :], bh[...], bl[...])
        row = lax.broadcasted_iota(jnp.int32, total.shape, 0)
        res[at, :] = total + jnp.where(row % 2 == 0, ends, -ends)

    for s in range(n):
        packed = jnp.zeros((part, LANES), jnp.float32)
        for q in range(reps):
            at = s * rows + q * part
            packed = jnp.where(grp == q, res[at : at + part, 2 * LANES :], packed)
        lg_ref[s] = packed
    for p in range(3):
        if p == 0:
            grads = stream(3) * res[:, :LANES]
        else:
            grads = res[:, LANES : 2 * LANES] * feature(3 - p)
        x = stream(p)
        total = taps[tap_count * p][None, :] * grads
        for lag in range(tap_count):
            line = jnp.sum(grads * later(x, lag), axis=0, keepdims=True)
            tg_ref[tap_count * p + lag : tap_count * p + lag + 1, :] = line * (1.0 / math.sqrt(tokens))
            if lag > 0:
                total = total + taps[tap_count * p + lag][None, :] * sooner(grads, lag)
        ig_ref[:, p] = total.astype(jnp.bfloat16).reshape(n, rows, LANES)


def collect_kernel(
    n, m, reps, ig_ref, lg_ref, tg_ref, out_ref, lo_ref, to_ref,
    ir, lr, l2, isend, irecv, lsend, lrecv, tsend, trecv, csend, crecv,
):
    me, mine = lax.axis_index("seq"), lax.axis_index("chan")
    meet([("seq", n), ("chan", m)])
    firsts, rest = [], []
    for j in range(1, n):
        peer = lax.rem(me + j, n)
        copy = pltpu.make_async_remote_copy(
            src_ref=lg_ref.at[peer], dst_ref=lr.at[me], send_sem=lsend.at[j - 1],
            recv_sem=lrecv.at[j - 1], device_id={"seq": peer}, device_id_type=MESH,
        )
        copy.start()
        firsts.append(copy)
    for j in range(1, n):
        peer = lax.rem(me + j, n)
        for src, dst, send, recv in (
            (ig_ref.at[peer], ir.at[me], isend, irecv), (tg_ref, to_ref.at[me], tsend, trecv)
        ):
            copy = pltpu.make_async_remote_copy(
                src_ref=src, dst_ref=dst, send_sem=send.at[j - 1],
                recv_sem=recv.at[j - 1], device_id={"seq": peer}, device_id_type=MESH,
            )
            copy.start()
            rest.append(copy)
    lr[me] = lg_ref[me]
    ir[me] = ig_ref[me]
    to_ref[me] = tg_ref[...]
    swap = swap_matrix(reps, LANES // reps)
    for copy in firsts:
        copy.wait()
    per = n // m
    seconds = []
    for j in range(1, m):
        peer = lax.rem(mine + j, m)
        copy = pltpu.make_async_remote_copy(
            src_ref=lr.at[pl.ds(peer * per, per)], dst_ref=l2.at[mine], send_sem=csend.at[j - 1],
            recv_sem=crecv.at[j - 1], device_id={"chan": peer}, device_id_type=MESH,
        )
        copy.start()
        seconds.append(copy)
    l2[mine] = lr[pl.ds(mine * per, per)]
    for copy in rest + seconds:
        copy.wait()
    total = l2[0]
    for k in range(1, m):
        total = total + l2[k]
    lo_ref[...] = total
    tiles = n // reps
    for h in range(tiles):
        for p in range(3):
            joined = jnp.concatenate([ir[h * reps + g, p] for g in range(reps)], axis=1)
            moved = jnp.dot(joined, swap, preferred_element_type=jnp.float32).astype(jnp.bfloat16)
            for r in range(reps):
                at = (r * tiles + h) * LANES
                out_ref[p, :, at : at + LANES] = moved[:, r * LANES : (r + 1) * LANES]


def dma(count):
    return pltpu.SemaphoreType.DMA((count,))


def whole_specs(count):
    return [pl.BlockSpec(memory_space=pltpu.VMEM)] * count


def params(which=None):
    if which is None:
        return pltpu.CompilerParams(vmem_limit_bytes=56 << 20)
    return pltpu.CompilerParams(collective_id=which, has_side_effects=True, vmem_limit_bytes=32 << 20)


def half_tables(tokens):
    step = 32
    col = np.arange(tokens)
    coarse = np.arange(tokens // step)[:, None] * step * col[None, :] % (2 * tokens)
    fine = np.arange(step)[:, None] * col[None, :] % (2 * tokens)
    out = []
    for index in (coarse, fine):
        phase = index * (math.pi / tokens)
        out += [np.cos(phase).astype(np.float32), np.sin(phase).astype(np.float32)]
    return out


def fast_shards(n, m, proj_in, taps, long_filter, out_grad):
    streams, rows, channels = proj_in.shape
    groups = long_filter.shape[1]
    reps = channels // groups
    width = groups // n
    part = rows // reps
    tokens = n * rows
    f32, bf16 = jnp.float32, jnp.bfloat16
    shape = jax.ShapeDtypeStruct
    lined = taps.reshape(streams * 3, reps, n, width).transpose(2, 0, 1, 3).reshape(n, -1, LANES)
    lined = jnp.pad(lined, ((0, 0), (0, 16 - streams * 3), (0, 0)))
    rb, fr = pl.pallas_call(
        functools.partial(spread_kernel, n, reps),
        out_shape=(shape((n, streams + 1, rows, LANES), bf16), shape((n, part, LANES), f32)),
        in_specs=whole_specs(3),
        out_specs=whole_specs(2),
        scratch_shapes=[
            pltpu.VMEM((n, streams + 1, rows, LANES), bf16), pltpu.VMEM((n, part, LANES), f32),
        ] + [dma(n - 1)] * 4,
        compiler_params=params(0),
    )(proj_in, out_grad, long_filter)
    ca, sa, cb, sb = half_tables(tokens)
    side = pltpu.VMEM((tokens, tokens), bf16)
    tall = pltpu.VMEM((tokens, 3 * LANES), bf16)
    ig, lg, tg = pl.pallas_call(
        functools.partial(layer_kernel, n, reps),
        out_shape=(
            shape((n, streams, rows, LANES), bf16), shape((n, part, LANES), f32), shape((16, LANES), f32),
        ),
        in_specs=whole_specs(7),
        out_specs=whole_specs(3),
        scratch_shapes=[side] * 4 + [tall] * 6 + [pltpu.VMEM((tokens, 3 * LANES), f32)],
        compiler_params=params(),
    )(rb, fr, lined, ca, sa, cb, sb)
    out, lo, to = pl.pallas_call(
        functools.partial(collect_kernel, n, m, reps),
        out_shape=(
            shape((streams, rows, channels), bf16), shape((n // m, part, LANES), f32), shape((n, 16, LANES), f32),
        ),
        in_specs=whole_specs(3),
        out_specs=whole_specs(3),
        scratch_shapes=[
            pltpu.VMEM((n, streams, rows, LANES), bf16), pltpu.VMEM((n, part, LANES), f32),
            pltpu.VMEM((m, n // m, part, LANES), f32),
        ] + [dma(n - 1)] * 6 + [dma(m - 1)] * 2,
        compiler_params=params(1),
    )(ig, lg, tg)
    long_grad = lo.reshape(n // m, part, reps, width).transpose(2, 1, 0, 3).reshape(rows, groups // m)
    tap_grad = to[:, : streams * 3].reshape(n, streams * 3, reps, width).transpose(1, 2, 0, 3)
    return (out, long_grad, tap_grad.reshape(streams, 3, channels))


def fits(n, m, proj_in, taps, long_filter, out_grad):
    streams, rows, channels = proj_in.shape
    groups = long_filter.shape[1]
    if channels % groups or groups % n or n % m or streams != 3 or taps.shape[1] != 3:
        return False
    reps, width = channels // groups, groups // n
    if reps < 2 or reps * width != LANES or n % reps or rows % (8 * reps) or rows % 16:
        return False
    return n * rows <= TABLE_LIMIT and n * rows % 256 == 0


def routed(n, m, *arrays):
    return fast_shards(n, m, *arrays) if fits(n, m, *arrays) else shards(*arrays)


def solution(mesh):
    return jax.shard_map(
        functools.partial(routed, mesh.shape["seq"], mesh.shape["chan"]),
        mesh=mesh,
        in_specs=(P(None, "seq", "chan"), P(None, None, "chan"), P("seq", None), P("seq", "chan")),
        out_specs=(P(None, "seq", "chan"), P("seq", "chan"), P(None, None, "chan")),
        check_vma=False,
    )
```

```python
import functools
import math

import jax
import jax.numpy as jnp
import numpy as np
from jax import lax
from jax.experimental import pallas as pl
from jax.experimental.pallas import tpu as pltpu
from jax.sharding import PartitionSpec as P

MESH = pl.DeviceIdType.MESH
LANES = 128
TABLE_LIMIT = 1024


def shifted(x, axis, by):
    devices = lax.axis_size(axis)
    pairs = [(i, i + by) for i in range(devices) if 0 <= i + by < devices]
    return lax.ppermute(x, axis, pairs)


def angle_table(left_index, right_index, period):
    product = left_index[:, None] * right_index[None, :] % period
    phase = product.astype(jnp.float32) * (2.0 * math.pi / period)
    return (jnp.cos(phase), jnp.sin(phase))


def contract(pattern, factor_table, operand):
    return jnp.einsum(pattern, factor_table, operand, precision=lax.Precision.HIGHEST)


def steps_of(count):
    return jnp.arange(count, dtype=jnp.int32)


def whole_forward(signal, seq_width):
    tok_rows, stack_count, channels = signal.shape
    period = 2 * seq_width * tok_rows
    narrow = channels // seq_width
    arrived = lax.all_to_all(signal, "seq", split_axis=2, concat_axis=0, tiled=True)
    laid = arrived.reshape(seq_width, tok_rows, stack_count, narrow).transpose(2, 3, 0, 1)
    cos_step, sin_step = angle_table(steps_of(2 * seq_width), steps_of(seq_width), 2 * seq_width)
    real_part = contract("qm,ncmj->ncqj", cos_step, laid)
    imag_part = -contract("qm,ncmj->ncqj", sin_step, laid)
    cos_turn, sin_turn = angle_table(steps_of(2 * seq_width), steps_of(tok_rows), period)
    turned_re = real_part * cos_turn + imag_part * sin_turn
    turned_im = imag_part * cos_turn - real_part * sin_turn
    cos_row, sin_row = angle_table(steps_of(tok_rows), steps_of(tok_rows), tok_rows)
    spec_re = contract("rj,ncqj->ncqr", cos_row, turned_re) + contract(
        "rj,ncqj->ncqr", sin_row, turned_im
    )
    spec_im = contract("rj,ncqj->ncqr", cos_row, turned_im) - contract(
        "rj,ncqj->ncqr", sin_row, turned_re
    )
    return (spec_re, spec_im)


def whole_inverse(spec_re, spec_im, seq_width):
    stack_count, narrow, freq_count, tok_rows = spec_re.shape
    period = 2 * seq_width * tok_rows
    cos_row, sin_row = angle_table(steps_of(tok_rows), steps_of(tok_rows), tok_rows)
    back_re = contract("rj,ncqr->ncqj", cos_row, spec_re) - contract(
        "rj,ncqr->ncqj", sin_row, spec_im
    )
    back_im = contract("rj,ncqr->ncqj", sin_row, spec_re) + contract(
        "rj,ncqr->ncqj", cos_row, spec_im
    )
    cos_turn, sin_turn = angle_table(steps_of(freq_count), steps_of(tok_rows), period)
    turned_re = back_re * cos_turn - back_im * sin_turn
    turned_im = back_re * sin_turn + back_im * cos_turn
    cos_step, sin_step = angle_table(steps_of(seq_width), steps_of(freq_count), freq_count)
    signal = contract("mq,ncqj->ncmj", cos_step, turned_re) - contract(
        "mq,ncqj->ncmj", sin_step, turned_im
    )
    signal = (
        (signal / period).transpose(2, 3, 0, 1).reshape(seq_width * tok_rows, stack_count, narrow)
    )
    return lax.all_to_all(signal, "seq", split_axis=0, concat_axis=2, tiled=True)


def member(values, index, stack_axis):
    return lax.index_in_dim(values, index, stack_axis, keepdims=False)


def shards(proj_in, taps, long_filter, out_grad):
    stream_count, tok_rows, channels = proj_in.shape
    tap_count = taps.shape[1]
    groups = long_filter.shape[1]
    seq_width = lax.axis_size("seq")
    lower_rim = shifted(proj_in[:, tok_rows - (tap_count - 1) :, :], "seq", 1)
    extended = jnp.concatenate([lower_rim, proj_in], axis=1).astype(jnp.float32)
    lagged = [
        extended[:, tap_count - 1 - lag_step : tap_count - 1 - lag_step + tok_rows, :]
        for lag_step in range(tap_count)
    ]
    featured = taps[:, 0, None, :] * lagged[0]
    for lag_step in range(1, tap_count):
        featured = featured + taps[:, lag_step, None, :] * lagged[lag_step]
    query_rows, key_rows, value_rows = (featured[0], featured[1], featured[2])
    mixed_rows = key_rows * value_rows
    upstream = out_grad.astype(jnp.float32)
    conv_grad = upstream * query_rows
    tiled_filter = jnp.tile(long_filter, (1, channels // groups))
    signals = jnp.stack([mixed_rows, conv_grad, tiled_filter], axis=1)
    data_re, data_im = whole_forward(signals, seq_width)
    stack_axis = 0
    mix_re, mix_im = (member(data_re, 0, stack_axis), member(data_im, 0, stack_axis))
    grad_re, grad_im = (member(data_re, 1, stack_axis), member(data_im, 1, stack_axis))
    filt_re, filt_im = (member(data_re, 2, stack_axis), member(data_im, 2, stack_axis))
    conv_re = filt_re * mix_re - filt_im * mix_im
    conv_im = filt_re * mix_im + filt_im * mix_re
    back_re = filt_re * grad_re + filt_im * grad_im
    back_im = filt_re * grad_im - filt_im * grad_re
    corr_re = grad_re * mix_re + grad_im * mix_im
    corr_im = grad_im * mix_re - grad_re * mix_im
    prod_re = jnp.stack([conv_re, back_re, corr_re], axis=stack_axis)
    prod_im = jnp.stack([conv_im, back_im, corr_im], axis=stack_axis)
    outputs = whole_inverse(prod_re, prod_im, seq_width)
    conv_out, mixed_grad = (outputs[:, 0], outputs[:, 1])
    filt_grad = jnp.sum(outputs[:, 2].reshape(tok_rows, channels // groups, groups), axis=1)
    long_grad = lax.psum_scatter(filt_grad, "chan", scatter_dimension=1, tiled=True)
    feature_grad = jnp.stack(
        [upstream * conv_out, mixed_grad * value_rows, mixed_grad * key_rows], axis=0
    )
    upper_rim = shifted(feature_grad[:, : tap_count - 1, :], "seq", -1)
    trailing = jnp.concatenate([feature_grad, upper_rim], axis=1)
    input_grad = taps[:, 0, None, :] * feature_grad
    for lag_step in range(1, tap_count):
        input_grad = (
            input_grad + taps[:, lag_step, None, :] * trailing[:, lag_step : lag_step + tok_rows]
        )
    partial_taps = jnp.stack(
        [jnp.sum(feature_grad * lagged[lag_step], axis=1) for lag_step in range(tap_count)], axis=1
    )
    tap_grad = lax.psum(partial_taps, "seq") / math.sqrt(seq_width * tok_rows)
    return (input_grad.astype(jnp.bfloat16), long_grad, tap_grad)


def meet(axis_sizes):
    barrier = pltpu.get_barrier_semaphore()
    total = 0
    for axis, size in axis_sizes:
        me = lax.axis_index(axis)
        for j in range(1, size):
            pl.semaphore_signal(
                barrier, inc=1, device_id={axis: lax.rem(me + j, size)}, device_id_type=MESH
            )
        total += size - 1
    pl.semaphore_wait(barrier, total)


def swap_matrix(reps, width):
    side = reps * LANES
    row = lax.broadcasted_iota(jnp.int32, (side, side), 0)
    col = lax.broadcasted_iota(jnp.int32, (side, side), 1)
    outer, inner, rest = row // LANES, (row % LANES) // width, row % width
    hit = inner * LANES + outer * width + rest == col
    return jnp.where(hit, 1.0, 0.0).astype(jnp.bfloat16)


def lane_group(rows, width):
    return lax.broadcasted_iota(jnp.int32, (rows, LANES), 1) // width


def turn(x, shift, axis):
    shift = shift % x.shape[axis]
    return x if shift == 0 else pltpu.roll(x, shift, axis)


def halves(x):
    high = x.astype(jnp.bfloat16)
    return high, (x - high.astype(jnp.float32)).astype(jnp.bfloat16)


def later(x, lag):
    if lag == 0:
        return x
    row = lax.broadcasted_iota(jnp.int32, x.shape, 0)
    return jnp.where(row < lag, 0.0, pltpu.roll(x, lag, 0))


def sooner(x, lag):
    if lag == 0:
        return x
    row = lax.broadcasted_iota(jnp.int32, x.shape, 0)
    return jnp.where(row >= x.shape[0] - lag, 0.0, pltpu.roll(x, x.shape[0] - lag, 0))


def group_sum(x, reps):
    total = x
    for r in range(1, reps):
        total = total + turn(x, r * (LANES // reps), 1)
    return total


def three(high, low, x_high, x_low):
    def dot(a, b):
        return jnp.dot(a, b, preferred_element_type=jnp.float32)

    return dot(high, x_high) + (dot(high, x_low) + dot(low, x_high))


def make_table(ca, sa, cb, sb, ch, cl, sh, sl):
    step = cb.shape[0]

    @pl.loop(0, ca.shape[0])
    def _(i):
        c0, s0 = ca[pl.ds(i, 1), :], sa[pl.ds(i, 1), :]
        rows = pl.ds(pl.multiple_of(i * step, step), step)
        ch[rows, :], cl[rows, :] = halves(c0 * cb[...] - s0 * sb[...])
        sh[rows, :], sl[rows, :] = halves(s0 * cb[...] + c0 * sb[...])


def whole_kernel(
    n, m, reps, x_ref, og_ref, lf_ref, tp_ref, ca, sa, cb, sb, out_ref, lo_ref, to_ref,
    xs, xr, fs, fr, ch, cl, sh, sl, mh, ml, gg, sa_f, sb_f, eh, el, oh, ol, ec, oc, res, res0,
    igs, igr, lgs, lgr, l2, tgs, tgr, sems, csems,
):
    me, mine = lax.axis_index("seq"), lax.axis_index("chan")
    width = LANES // reps
    streams, rows, _ = x_ref.shape
    tap_count = tp_ref.shape[1]
    tokens = n * rows
    part = rows // reps
    tiles = n // reps
    meet([("seq", n), ("chan", m)])
    grp = lane_group(part, width)

    def ship(kind, source, target):
        copies = []
        for j in range(1, n):
            peer = lax.rem(me + j, n)
            copy = pltpu.make_async_remote_copy(
                src_ref=source(peer), dst_ref=target, send_sem=sems.at[0, kind, j - 1],
                recv_sem=sems.at[1, kind, j - 1], device_id={"seq": peer}, device_id_type=MESH,
            )
            copy.start()
            copies.append(copy)
        return copies

    swap = swap_matrix(reps, width)

    def gather_stream(source, place):
        for h in range(tiles):
            joined = jnp.concatenate(
                [source[:, (r * tiles + h) * LANES : (r * tiles + h + 1) * LANES] for r in range(reps)],
                axis=1,
            )
            moved = jnp.dot(joined, swap, preferred_element_type=jnp.float32).astype(jnp.bfloat16)
            for g in range(reps):
                xs[place // 2, h * reps + g, place % 2] = moved[:, g * LANES : (g + 1) * LANES]

    gather_stream(x_ref.at[1], 0)
    gather_stream(x_ref.at[2], 1)
    first = ship(0, lambda peer: xs.at[0, peer], xr.at[0, me])
    for s in range(n):
        base = (s // reps) * LANES
        packed = jnp.zeros((part, LANES), jnp.float32)
        for q in range(reps):
            tile = lf_ref[q * part : (q + 1) * part, base : base + LANES]
            packed = jnp.where(grp == q, turn(tile, (q - s % reps) * width, 1), packed)
        fs[s] = packed
    first += ship(1, lambda peer: fs.at[peer], fr.at[me])
    gather_stream(x_ref.at[0], 2)
    gather_stream(og_ref, 3)
    second = ship(2, lambda peer: xs.at[1, peer], xr.at[1, me])
    xr[0, me] = xs[0, me]
    xr[1, me] = xs[1, me]
    fr[me] = fs[me]

    taps = []
    home, slot = me // reps, lax.rem(me, reps)
    for p in range(streams):
        mixed_taps = jnp.zeros((tap_count, LANES), jnp.float32)
        for r in range(reps):
            at = pl.multiple_of((r * tiles + home) * LANES, LANES)
            tile = tp_ref[p, :, pl.ds(at, LANES)]
            shift = lax.rem((r + reps - slot) * width, LANES)
            mixed_taps = jnp.where(
                lane_group(tap_count, width) == r, pltpu.roll(tile, shift, 1), mixed_taps
            )
        taps.append([mixed_taps[i : i + 1] for i in range(tap_count)])
    tgs[...] = jnp.zeros_like(tgs)
    make_table(ca, sa, cb, sb, ch, cl, sh, sl)

    places = {1: (0, 0), 2: (0, 1), 0: (1, 0), 3: (1, 1)}

    def stream(p):
        half, at = places[p]
        return xr[half, :, at].reshape(tokens, LANES).astype(jnp.float32)

    def feature(p):
        x = stream(p)
        total = taps[p][0] * x
        for lag in range(1, tap_count):
            total = total + taps[p][lag] * later(x, lag)
        return total

    def alternating(count):
        row = lax.broadcasted_iota(jnp.int32, (count, LANES), 0)
        return jnp.where(row % 2 == 0, 1.0, -1.0)

    def dot(left, right):
        return jnp.dot(left, right, preferred_element_type=jnp.float32)

    def paired(high, low, both):
        wide = dot(high, both[...])
        return wide[:, :LANES] + (wide[:, LANES:] + dot(low, both[:, :LANES]))

    def weight_of(i, count):
        row = lax.broadcasted_iota(jnp.int32, (count, LANES), 0) + i * count
        return jnp.where(row == 0, 0.5 / tokens, 1.0 / tokens)

    for copy in first:
        copy.wait()
    sign = alternating(tokens)
    mixed = feature(1) * feature(2)
    mh[:, :LANES], ml[:, :LANES] = halves(mixed)
    mixed_end = jnp.sum(sign * mixed, axis=0, keepdims=True)
    filt_end = jnp.zeros((1, LANES), jnp.float32)
    for s in range(n):
        packed = fr[s]
        for q in range(reps):
            piece = group_sum(jnp.where(grp == q, packed, 0.0), reps)
            filt_end = filt_end + jnp.sum(alternating(part) * piece, axis=0, keepdims=True)
            at = s * rows + q * part
            mh[at : at + part, LANES:], ml[at : at + part, LANES:] = halves(piece)
    chunk = min(256, tokens)

    @pl.loop(0, tokens // chunk)
    def _(i):
        at = pl.ds(pl.multiple_of(i * chunk, chunk), chunk)
        a = three(ch[at, :], cl[at, :], mh[...], ml[...])
        b = three(sh[at, :], sl[at, :], mh[...], ml[...])
        sa_f[at, :], sb_f[at, :] = a, b
        am, af, bm, bf = a[:, :LANES], a[:, LANES:], b[:, :LANES], b[:, LANES:]
        weight = weight_of(i, chunk)
        ec[at, :LANES], ec[at, LANES:] = halves((af * am - bf * bm) * weight)
        oc[at, :LANES], oc[at, LANES:] = halves((af * bm + bf * am) * weight)

    for copy in second:
        copy.wait()
    grad = stream(3) * feature(0)
    gg[:, :LANES], gg[:, LANES:] = halves(grad)
    grad_end = jnp.sum(sign * grad, axis=0, keepdims=True)

    @pl.loop(0, tokens // chunk)
    def _(i):
        at = pl.ds(pl.multiple_of(i * chunk, chunk), chunk)
        ag = paired(ch[at, :], cl[at, :], gg)
        bg = paired(sh[at, :], sl[at, :], gg)
        am, af, bm, bf = sa_f[at, :LANES], sa_f[at, LANES:], sb_f[at, :LANES], sb_f[at, LANES:]
        weight = weight_of(i, chunk)
        eh[at, :LANES], el[at, :LANES] = halves((af * ag + bf * bg) * weight)
        oh[at, :LANES], ol[at, :LANES] = halves((af * bg - bf * ag) * weight)
        eh[at, LANES:], el[at, LANES:] = halves(group_sum(ag * am + bg * bm, reps) * weight)
        oh[at, LANES:], ol[at, LANES:] = halves(group_sum(bg * am - ag * bm, reps) * weight)

    ends = jnp.concatenate(
        [filt_end * grad_end, group_sum(grad_end * mixed_end, reps)], axis=1
    ) * (0.5 / tokens)
    conv_end = filt_end * mixed_end * (0.5 / tokens)

    @pl.loop(0, tokens // chunk)
    def _(i):
        at = pl.ds(pl.multiple_of(i * chunk, chunk), chunk)
        total = three(ch[at, :], cl[at, :], eh[...], el[...])
        total = total + three(sh[at, :], sl[at, :], oh[...], ol[...])
        row = lax.broadcasted_iota(jnp.int32, total.shape, 0)
        res[at, :] = total + jnp.where(row % 2 == 0, ends, -ends)

    def finish(p, grads, place):
        total = taps[p][0] * grads
        for lag in range(1, tap_count):
            total = total + taps[p][lag] * sooner(grads, lag)
        place[...] = total.astype(jnp.bfloat16).reshape(n, rows, LANES)

    def tap_lines(p, grads):
        x = stream(p)
        for lag in range(tap_count):
            line = jnp.sum(grads * later(x, lag), axis=0, keepdims=True)
            tgs[tap_count * p + lag : tap_count * p + lag + 1, :] = line * (1.0 / math.sqrt(tokens))

    for s in range(n):
        packed = jnp.zeros((part, LANES), jnp.float32)
        for q in range(reps):
            at = s * rows + q * part
            packed = jnp.where(grp == q, res[at : at + part, LANES:], packed)
        lgs[s] = packed
    long_sent = ship(3, lambda peer: lgs.at[peer], lgr.at[me])
    lgr[me] = lgs[me]
    key_grads = res[:, :LANES] * feature(2)
    finish(1, key_grads, igs.at[1])
    key_sent = ship(4, lambda peer: igs.at[1, peer], igr.at[1, me])
    value_grads = res[:, :LANES] * feature(1)
    finish(2, value_grads, igs.at[2])
    value_sent = ship(5, lambda peer: igs.at[2, peer], igr.at[2, me])

    @pl.loop(0, tokens // chunk)
    def _(i):
        at = pl.ds(pl.multiple_of(i * chunk, chunk), chunk)
        total = paired(ch[at, :], cl[at, :], ec) + paired(sh[at, :], sl[at, :], oc)
        row = lax.broadcasted_iota(jnp.int32, total.shape, 0)
        res0[at, :] = total + jnp.where(row % 2 == 0, conv_end, -conv_end)

    query_grads = stream(3) * res0[...]
    finish(0, query_grads, igs.at[0])
    query_sent = ship(6, lambda peer: igs.at[0, peer], igr.at[0, me])
    tap_lines(0, query_grads)
    tap_lines(1, res[:, :LANES] * feature(2))
    tap_lines(2, res[:, :LANES] * feature(1))
    taps_sent = ship(7, lambda peer: tgs, tgr.at[me])
    tgr[me] = tgs[...]
    for p in range(streams):
        igr[p, me] = igs[p, me]
    for copy in long_sent:
        copy.wait()
    per = n // m
    chan_sent = []
    for j in range(1, m):
        peer = lax.rem(mine + j, m)
        copy = pltpu.make_async_remote_copy(
            src_ref=lgr.at[pl.ds(peer * per, per)], dst_ref=l2.at[mine], send_sem=csems.at[0, j - 1],
            recv_sem=csems.at[1, j - 1], device_id={"chan": peer}, device_id_type=MESH,
        )
        copy.start()
        chan_sent.append(copy)
    l2[mine] = lgr[pl.ds(mine * per, per)]

    def put_stream(p):
        for h in range(tiles):
            joined = jnp.concatenate([igr[p, h * reps + g] for g in range(reps)], axis=1)
            moved = dot(joined, swap).astype(jnp.bfloat16)
            for r in range(reps):
                at = (r * tiles + h) * LANES
                out_ref[p, :, at : at + LANES] = moved[:, r * LANES : (r + 1) * LANES]

    for copy in key_sent:
        copy.wait()
    put_stream(1)
    for copy in value_sent:
        copy.wait()
    put_stream(2)
    for copy in chan_sent:
        copy.wait()
    total = l2[0]
    for k in range(1, m):
        total = total + l2[k]
    for q in range(reps):
        line = jnp.zeros((part, LANES), jnp.float32)
        for k in range(per):
            line = jnp.where(grp == k, turn(total[k], (k - q) * width, 1), line)
        lo_ref[q * part : (q + 1) * part, :] = line[:, : per * width]
    for copy in query_sent:
        copy.wait()
    put_stream(0)
    for copy in taps_sent:
        copy.wait()
    for h in range(tiles):
        for r in range(reps):
            line = jnp.zeros((16, LANES), jnp.float32)
            for g in range(reps):
                moved = turn(tgr[h * reps + g], (g - r) * width, 1)
                line = jnp.where(lane_group(16, width) == g, moved, line)
            at = (r * tiles + h) * LANES
            for p in range(streams):
                to_ref[p, :, at : at + LANES] = line[tap_count * p : tap_count * (p + 1)]


def whole_specs(count):
    return [pl.BlockSpec(memory_space=pltpu.VMEM)] * count


def half_tables(tokens):
    step = 32
    col = np.arange(tokens)
    coarse = np.arange(tokens // step)[:, None] * step * col[None, :] % (2 * tokens)
    fine = np.arange(step)[:, None] * col[None, :] % (2 * tokens)
    out = []
    for index in (coarse, fine):
        phase = index * (math.pi / tokens)
        out += [np.cos(phase).astype(np.float32), np.sin(phase).astype(np.float32)]
    return out


def fast_shards(n, m, proj_in, taps, long_filter, out_grad):
    streams, rows, channels = proj_in.shape
    groups = long_filter.shape[1]
    reps = channels // groups
    part = rows // reps
    tokens = n * rows
    f32, bf16 = jnp.float32, jnp.bfloat16
    shape, vmem = jax.ShapeDtypeStruct, pltpu.VMEM
    wide = vmem((tokens, 2 * LANES), bf16)
    full = vmem((tokens, 2 * LANES), f32)
    packs = vmem((n, part, LANES), f32)
    moved = vmem((2, n, 2, rows, LANES), bf16)
    grads = vmem((streams, n, rows, LANES), bf16)
    return pl.pallas_call(
        functools.partial(whole_kernel, n, m, reps),
        out_shape=(
            shape((streams, rows, channels), bf16), shape((rows, groups // m), f32), shape(taps.shape, f32),
        ),
        in_specs=whole_specs(8),
        out_specs=whole_specs(3),
        scratch_shapes=[moved, moved, packs, packs]
        + [vmem((tokens, tokens), bf16)] * 4
        + [wide] * 3 + [full] * 2 + [wide] * 6 + [full, vmem((tokens, LANES), f32)]
        + [grads, grads, packs, packs, vmem((m, n // m, part, LANES), f32)]
        + [vmem((16, LANES), f32), vmem((n, 16, LANES), f32)]
        + [pltpu.SemaphoreType.DMA((2, 8, n - 1)), pltpu.SemaphoreType.DMA((2, m - 1))],
        compiler_params=pltpu.CompilerParams(
            collective_id=0, has_side_effects=True, vmem_limit_bytes=56 << 20
        ),
    )(proj_in, out_grad, long_filter, taps, *half_tables(tokens))


def fits(n, m, proj_in, taps, long_filter, out_grad):
    streams, rows, channels = proj_in.shape
    groups = long_filter.shape[1]
    if channels % groups or groups % n or n % m or streams != 3 or taps.shape[1] != 3:
        return False
    reps, width = channels // groups, groups // n
    if reps < 2 or reps * width != LANES or n % reps or rows % (8 * reps) or rows % 16:
        return False
    return n * rows <= TABLE_LIMIT and n * rows % 256 == 0


def routed(n, m, *arrays):
    return fast_shards(n, m, *arrays) if fits(n, m, *arrays) else shards(*arrays)


def solution(mesh):
    return jax.shard_map(
        functools.partial(routed, mesh.shape["seq"], mesh.shape["chan"]),
        mesh=mesh,
        in_specs=(P(None, "seq", "chan"), P(None, None, "chan"), P("seq", None), P("seq", "chan")),
        out_specs=(P(None, "seq", "chan"), P("seq", "chan"), P(None, None, "chan")),
        check_vma=False,
    )
```

```python
import functools
import math

import jax
import jax.numpy as jnp
import numpy as np
from jax import lax
from jax.experimental import pallas as pl
from jax.experimental.pallas import tpu as pltpu
from jax.sharding import PartitionSpec as P

MESH = pl.DeviceIdType.MESH
LANES = 128
TABLE_LIMIT = 1024


def shifted(x, axis, by):
    devices = lax.axis_size(axis)
    pairs = [(i, i + by) for i in range(devices) if 0 <= i + by < devices]
    return lax.ppermute(x, axis, pairs)


def angle_table(left_index, right_index, period):
    product = left_index[:, None] * right_index[None, :] % period
    phase = product.astype(jnp.float32) * (2.0 * math.pi / period)
    return (jnp.cos(phase), jnp.sin(phase))


def contract(pattern, factor_table, operand):
    return jnp.einsum(pattern, factor_table, operand, precision=lax.Precision.HIGHEST)


def steps_of(count):
    return jnp.arange(count, dtype=jnp.int32)


def whole_forward(signal, seq_width):
    tok_rows, stack_count, channels = signal.shape
    period = 2 * seq_width * tok_rows
    narrow = channels // seq_width
    arrived = lax.all_to_all(signal, "seq", split_axis=2, concat_axis=0, tiled=True)
    laid = arrived.reshape(seq_width, tok_rows, stack_count, narrow).transpose(2, 3, 0, 1)
    cos_step, sin_step = angle_table(steps_of(2 * seq_width), steps_of(seq_width), 2 * seq_width)
    real_part = contract("qm,ncmj->ncqj", cos_step, laid)
    imag_part = -contract("qm,ncmj->ncqj", sin_step, laid)
    cos_turn, sin_turn = angle_table(steps_of(2 * seq_width), steps_of(tok_rows), period)
    turned_re = real_part * cos_turn + imag_part * sin_turn
    turned_im = imag_part * cos_turn - real_part * sin_turn
    cos_row, sin_row = angle_table(steps_of(tok_rows), steps_of(tok_rows), tok_rows)
    spec_re = contract("rj,ncqj->ncqr", cos_row, turned_re) + contract(
        "rj,ncqj->ncqr", sin_row, turned_im
    )
    spec_im = contract("rj,ncqj->ncqr", cos_row, turned_im) - contract(
        "rj,ncqj->ncqr", sin_row, turned_re
    )
    return (spec_re, spec_im)


def whole_inverse(spec_re, spec_im, seq_width):
    stack_count, narrow, freq_count, tok_rows = spec_re.shape
    period = 2 * seq_width * tok_rows
    cos_row, sin_row = angle_table(steps_of(tok_rows), steps_of(tok_rows), tok_rows)
    back_re = contract("rj,ncqr->ncqj", cos_row, spec_re) - contract(
        "rj,ncqr->ncqj", sin_row, spec_im
    )
    back_im = contract("rj,ncqr->ncqj", sin_row, spec_re) + contract(
        "rj,ncqr->ncqj", cos_row, spec_im
    )
    cos_turn, sin_turn = angle_table(steps_of(freq_count), steps_of(tok_rows), period)
    turned_re = back_re * cos_turn - back_im * sin_turn
    turned_im = back_re * sin_turn + back_im * cos_turn
    cos_step, sin_step = angle_table(steps_of(seq_width), steps_of(freq_count), freq_count)
    signal = contract("mq,ncqj->ncmj", cos_step, turned_re) - contract(
        "mq,ncqj->ncmj", sin_step, turned_im
    )
    signal = (
        (signal / period).transpose(2, 3, 0, 1).reshape(seq_width * tok_rows, stack_count, narrow)
    )
    return lax.all_to_all(signal, "seq", split_axis=0, concat_axis=2, tiled=True)


def member(values, index, stack_axis):
    return lax.index_in_dim(values, index, stack_axis, keepdims=False)


def shards(proj_in, taps, long_filter, out_grad):
    stream_count, tok_rows, channels = proj_in.shape
    tap_count = taps.shape[1]
    groups = long_filter.shape[1]
    seq_width = lax.axis_size("seq")
    lower_rim = shifted(proj_in[:, tok_rows - (tap_count - 1) :, :], "seq", 1)
    extended = jnp.concatenate([lower_rim, proj_in], axis=1).astype(jnp.float32)
    lagged = [
        extended[:, tap_count - 1 - lag_step : tap_count - 1 - lag_step + tok_rows, :]
        for lag_step in range(tap_count)
    ]
    featured = taps[:, 0, None, :] * lagged[0]
    for lag_step in range(1, tap_count):
        featured = featured + taps[:, lag_step, None, :] * lagged[lag_step]
    query_rows, key_rows, value_rows = (featured[0], featured[1], featured[2])
    mixed_rows = key_rows * value_rows
    upstream = out_grad.astype(jnp.float32)
    conv_grad = upstream * query_rows
    tiled_filter = jnp.tile(long_filter, (1, channels // groups))
    signals = jnp.stack([mixed_rows, conv_grad, tiled_filter], axis=1)
    data_re, data_im = whole_forward(signals, seq_width)
    stack_axis = 0
    mix_re, mix_im = (member(data_re, 0, stack_axis), member(data_im, 0, stack_axis))
    grad_re, grad_im = (member(data_re, 1, stack_axis), member(data_im, 1, stack_axis))
    filt_re, filt_im = (member(data_re, 2, stack_axis), member(data_im, 2, stack_axis))
    conv_re = filt_re * mix_re - filt_im * mix_im
    conv_im = filt_re * mix_im + filt_im * mix_re
    back_re = filt_re * grad_re + filt_im * grad_im
    back_im = filt_re * grad_im - filt_im * grad_re
    corr_re = grad_re * mix_re + grad_im * mix_im
    corr_im = grad_im * mix_re - grad_re * mix_im
    prod_re = jnp.stack([conv_re, back_re, corr_re], axis=stack_axis)
    prod_im = jnp.stack([conv_im, back_im, corr_im], axis=stack_axis)
    outputs = whole_inverse(prod_re, prod_im, seq_width)
    conv_out, mixed_grad = (outputs[:, 0], outputs[:, 1])
    filt_grad = jnp.sum(outputs[:, 2].reshape(tok_rows, channels // groups, groups), axis=1)
    long_grad = lax.psum_scatter(filt_grad, "chan", scatter_dimension=1, tiled=True)
    feature_grad = jnp.stack(
        [upstream * conv_out, mixed_grad * value_rows, mixed_grad * key_rows], axis=0
    )
    upper_rim = shifted(feature_grad[:, : tap_count - 1, :], "seq", -1)
    trailing = jnp.concatenate([feature_grad, upper_rim], axis=1)
    input_grad = taps[:, 0, None, :] * feature_grad
    for lag_step in range(1, tap_count):
        input_grad = (
            input_grad + taps[:, lag_step, None, :] * trailing[:, lag_step : lag_step + tok_rows]
        )
    partial_taps = jnp.stack(
        [jnp.sum(feature_grad * lagged[lag_step], axis=1) for lag_step in range(tap_count)], axis=1
    )
    tap_grad = lax.psum(partial_taps, "seq") / math.sqrt(seq_width * tok_rows)
    return (input_grad.astype(jnp.bfloat16), long_grad, tap_grad)


def meet(axis_sizes):
    barrier = pltpu.get_barrier_semaphore()
    total = 0
    for axis, size in axis_sizes:
        me = lax.axis_index(axis)
        for j in range(1, size):
            pl.semaphore_signal(
                barrier, inc=1, device_id={axis: lax.rem(me + j, size)}, device_id_type=MESH
            )
        total += size - 1
    pl.semaphore_wait(barrier, total)


def swap_matrix(reps, width):
    side = reps * LANES
    row = lax.broadcasted_iota(jnp.int32, (side, side), 0)
    col = lax.broadcasted_iota(jnp.int32, (side, side), 1)
    outer, inner, rest = row // LANES, (row % LANES) // width, row % width
    hit = inner * LANES + outer * width + rest == col
    return jnp.where(hit, 1.0, 0.0).astype(jnp.bfloat16)


def lane_group(rows, width):
    return lax.broadcasted_iota(jnp.int32, (rows, LANES), 1) // width


def turn(x, shift, axis):
    shift = shift % x.shape[axis]
    return x if shift == 0 else pltpu.roll(x, shift, axis)


def halves(x):
    high = x.astype(jnp.bfloat16)
    return high, (x - high.astype(jnp.float32)).astype(jnp.bfloat16)


def later(x, lag):
    if lag == 0:
        return x
    row = lax.broadcasted_iota(jnp.int32, x.shape, 0)
    return jnp.where(row < lag, 0.0, pltpu.roll(x, lag, 0))


def sooner(x, lag):
    if lag == 0:
        return x
    row = lax.broadcasted_iota(jnp.int32, x.shape, 0)
    return jnp.where(row >= x.shape[0] - lag, 0.0, pltpu.roll(x, x.shape[0] - lag, 0))


def group_sum(x, reps):
    total = x
    for r in range(1, reps):
        total = total + turn(x, r * (LANES // reps), 1)
    return total


def three(high, low, x_high, x_low):
    def dot(a, b):
        return jnp.dot(a, b, preferred_element_type=jnp.float32)

    return dot(high, x_high) + (dot(high, x_low) + dot(low, x_high))


def make_table(ca, sa, cb, sb, ch, cl, sh, sl):
    step = cb.shape[0]

    @pl.loop(0, ca.shape[0])
    def _(i):
        c0, s0 = ca[pl.ds(i, 1), :], sa[pl.ds(i, 1), :]
        rows = pl.ds(pl.multiple_of(i * step, step), step)
        ch[rows, :], cl[rows, :] = halves(c0 * cb[...] - s0 * sb[...])
        sh[rows, :], sl[rows, :] = halves(s0 * cb[...] + c0 * sb[...])


def whole_kernel(
    n, m, reps, x_ref, og_ref, lf_ref, tp_ref, ca, sa, cb, sb, out_ref, lo_ref, to_ref,
    xs, xr, fs, fr, ch, cl, sh, sl, mh, ml, gg, sa_f, sb_f, eh, el, oh, ol, ec, oc, res, res0,
    igs, igr, lgs, lgr, l2, tgs, tgr, sems, csems,
):
    me, mine = lax.axis_index("seq"), lax.axis_index("chan")
    width = LANES // reps
    streams, rows, _ = x_ref.shape
    tap_count = tp_ref.shape[1]
    tokens = n * rows
    part = rows // reps
    tiles = n // reps
    meet([("seq", n), ("chan", m)])
    grp = lane_group(part, width)

    def ship(kind, source, target):
        copies = []
        for j in range(1, n):
            peer = lax.rem(me + j, n)
            copy = pltpu.make_async_remote_copy(
                src_ref=source(peer), dst_ref=target, send_sem=sems.at[0, kind, j - 1],
                recv_sem=sems.at[1, kind, j - 1], device_id={"seq": peer}, device_id_type=MESH,
            )
            copy.start()
            copies.append(copy)
        return copies

    swap = swap_matrix(reps, width)

    def gather_stream(source, place):
        for h in range(tiles):
            joined = jnp.concatenate(
                [source[:, (r * tiles + h) * LANES : (r * tiles + h + 1) * LANES] for r in range(reps)],
                axis=1,
            )
            moved = jnp.dot(joined, swap, preferred_element_type=jnp.float32).astype(jnp.bfloat16)
            for g in range(reps):
                xs[place // 2, h * reps + g, place % 2] = moved[:, g * LANES : (g + 1) * LANES]

    gather_stream(x_ref.at[0], 0)
    gather_stream(og_ref, 1)
    first = ship(0, lambda peer: xs.at[0, peer], xr.at[0, me])
    for s in range(n):
        base = (s // reps) * LANES
        packed = jnp.zeros((part, LANES), jnp.float32)
        for q in range(reps):
            tile = lf_ref[q * part : (q + 1) * part, base : base + LANES]
            packed = jnp.where(grp == q, turn(tile, (q - s % reps) * width, 1), packed)
        fs[s] = packed
    first += ship(1, lambda peer: fs.at[peer], fr.at[me])
    gather_stream(x_ref.at[1], 2)
    gather_stream(x_ref.at[2], 3)
    second = ship(2, lambda peer: xs.at[1, peer], xr.at[1, me])
    xr[0, me] = xs[0, me]
    xr[1, me] = xs[1, me]
    fr[me] = fs[me]

    taps = []
    home, slot = me // reps, lax.rem(me, reps)
    for p in range(streams):
        mixed_taps = jnp.zeros((tap_count, LANES), jnp.float32)
        for r in range(reps):
            at = pl.multiple_of((r * tiles + home) * LANES, LANES)
            tile = tp_ref[p, :, pl.ds(at, LANES)]
            shift = lax.rem((r + reps - slot) * width, LANES)
            mixed_taps = jnp.where(
                lane_group(tap_count, width) == r, pltpu.roll(tile, shift, 1), mixed_taps
            )
        taps.append([mixed_taps[i : i + 1] for i in range(tap_count)])
    tgs[...] = jnp.zeros_like(tgs)
    make_table(ca, sa, cb, sb, ch, cl, sh, sl)

    places = {0: (0, 0), 3: (0, 1), 1: (1, 0), 2: (1, 1)}

    def stream(p):
        half, at = places[p]
        return xr[half, :, at].reshape(tokens, LANES).astype(jnp.float32)

    def feature(p):
        x = stream(p)
        total = taps[p][0] * x
        for lag in range(1, tap_count):
            total = total + taps[p][lag] * later(x, lag)
        return total

    def alternating(count):
        row = lax.broadcasted_iota(jnp.int32, (count, LANES), 0)
        return jnp.where(row % 2 == 0, 1.0, -1.0)

    def dot(left, right):
        return jnp.dot(left, right, preferred_element_type=jnp.float32)

    def paired(high, low, both):
        wide = dot(high, both[...])
        return wide[:, :LANES] + (wide[:, LANES:] + dot(low, both[:, :LANES]))

    def weight_of(i, count):
        row = lax.broadcasted_iota(jnp.int32, (count, LANES), 0) + i * count
        return jnp.where(row == 0, 0.5 / tokens, 1.0 / tokens)

    for copy in first:
        copy.wait()
    sign = alternating(tokens)
    grad = stream(3) * feature(0)
    mh[:, :LANES], ml[:, :LANES] = halves(grad)
    grad_end = jnp.sum(sign * grad, axis=0, keepdims=True)
    filt_end = jnp.zeros((1, LANES), jnp.float32)
    for s in range(n):
        packed = fr[s]
        for q in range(reps):
            piece = group_sum(jnp.where(grp == q, packed, 0.0), reps)
            filt_end = filt_end + jnp.sum(alternating(part) * piece, axis=0, keepdims=True)
            at = s * rows + q * part
            mh[at : at + part, LANES:], ml[at : at + part, LANES:] = halves(piece)
    chunk = min(256, tokens)

    @pl.loop(0, tokens // chunk)
    def _(i):
        at = pl.ds(pl.multiple_of(i * chunk, chunk), chunk)
        a = three(ch[at, :], cl[at, :], mh[...], ml[...])
        b = three(sh[at, :], sl[at, :], mh[...], ml[...])
        sa_f[at, :], sb_f[at, :] = a, b
        ag, af, bg, bf = a[:, :LANES], a[:, LANES:], b[:, :LANES], b[:, LANES:]
        weight = weight_of(i, chunk)
        ec[at, :LANES], ec[at, LANES:] = halves((af * ag + bf * bg) * weight)
        oc[at, :LANES], oc[at, LANES:] = halves((af * bg - bf * ag) * weight)

    back_end = filt_end * grad_end * (0.5 / tokens)

    @pl.loop(0, tokens // chunk)
    def _(i):
        at = pl.ds(pl.multiple_of(i * chunk, chunk), chunk)
        total = paired(ch[at, :], cl[at, :], ec) + paired(sh[at, :], sl[at, :], oc)
        row = lax.broadcasted_iota(jnp.int32, total.shape, 0)
        res0[at, :] = total + jnp.where(row % 2 == 0, back_end, -back_end)

    for copy in second:
        copy.wait()

    def finish(p, grads, place):
        total = taps[p][0] * grads
        for lag in range(1, tap_count):
            total = total + taps[p][lag] * sooner(grads, lag)
        place[...] = total.astype(jnp.bfloat16).reshape(n, rows, LANES)

    def tap_lines(p, grads):
        x = stream(p)
        for lag in range(tap_count):
            line = jnp.sum(grads * later(x, lag), axis=0, keepdims=True)
            tgs[tap_count * p + lag : tap_count * p + lag + 1, :] = line * (1.0 / math.sqrt(tokens))

    key_rows, value_rows = feature(1), feature(2)
    mixed = key_rows * value_rows
    gg[:, :LANES], gg[:, LANES:] = halves(mixed)
    mixed_end = jnp.sum(sign * mixed, axis=0, keepdims=True)
    finish(1, res0[...] * value_rows, igs.at[1])
    key_sent = ship(4, lambda peer: igs.at[1, peer], igr.at[1, me])
    finish(2, res0[...] * key_rows, igs.at[2])
    value_sent = ship(5, lambda peer: igs.at[2, peer], igr.at[2, me])

    @pl.loop(0, tokens // chunk)
    def _(i):
        at = pl.ds(pl.multiple_of(i * chunk, chunk), chunk)
        am = paired(ch[at, :], cl[at, :], gg)
        bm = paired(sh[at, :], sl[at, :], gg)
        ag, af, bg, bf = sa_f[at, :LANES], sa_f[at, LANES:], sb_f[at, :LANES], sb_f[at, LANES:]
        weight = weight_of(i, chunk)
        eh[at, :LANES], el[at, :LANES] = halves((af * am - bf * bm) * weight)
        oh[at, :LANES], ol[at, :LANES] = halves((af * bm + bf * am) * weight)
        eh[at, LANES:], el[at, LANES:] = halves(group_sum(ag * am + bg * bm, reps) * weight)
        oh[at, LANES:], ol[at, LANES:] = halves(group_sum(bg * am - ag * bm, reps) * weight)

    ends = jnp.concatenate(
        [filt_end * mixed_end, group_sum(grad_end * mixed_end, reps)], axis=1
    ) * (0.5 / tokens)

    @pl.loop(0, tokens // chunk)
    def _(i):
        at = pl.ds(pl.multiple_of(i * chunk, chunk), chunk)
        total = three(ch[at, :], cl[at, :], eh[...], el[...])
        total = total + three(sh[at, :], sl[at, :], oh[...], ol[...])
        row = lax.broadcasted_iota(jnp.int32, total.shape, 0)
        res[at, :] = total + jnp.where(row % 2 == 0, ends, -ends)

    for s in range(n):
        packed = jnp.zeros((part, LANES), jnp.float32)
        for q in range(reps):
            at = s * rows + q * part
            packed = jnp.where(grp == q, res[at : at + part, LANES:], packed)
        lgs[s] = packed
    long_sent = ship(3, lambda peer: lgs.at[peer], lgr.at[me])
    lgr[me] = lgs[me]
    query_grads = stream(3) * res[:, :LANES]
    finish(0, query_grads, igs.at[0])
    query_sent = ship(6, lambda peer: igs.at[0, peer], igr.at[0, me])
    tap_lines(0, query_grads)
    tap_lines(1, res0[...] * feature(2))
    tap_lines(2, res0[...] * feature(1))
    taps_sent = ship(7, lambda peer: tgs, tgr.at[me])
    tgr[me] = tgs[...]
    for p in range(streams):
        igr[p, me] = igs[p, me]
    for copy in long_sent:
        copy.wait()
    per = n // m
    chan_sent = []
    for j in range(1, m):
        peer = lax.rem(mine + j, m)
        copy = pltpu.make_async_remote_copy(
            src_ref=lgr.at[pl.ds(peer * per, per)], dst_ref=l2.at[mine], send_sem=csems.at[0, j - 1],
            recv_sem=csems.at[1, j - 1], device_id={"chan": peer}, device_id_type=MESH,
        )
        copy.start()
        chan_sent.append(copy)
    l2[mine] = lgr[pl.ds(mine * per, per)]

    def put_stream(p):
        for h in range(tiles):
            joined = jnp.concatenate([igr[p, h * reps + g] for g in range(reps)], axis=1)
            moved = dot(joined, swap).astype(jnp.bfloat16)
            for r in range(reps):
                at = (r * tiles + h) * LANES
                out_ref[p, :, at : at + LANES] = moved[:, r * LANES : (r + 1) * LANES]

    for copy in key_sent:
        copy.wait()
    put_stream(1)
    for copy in value_sent:
        copy.wait()
    put_stream(2)
    for copy in chan_sent:
        copy.wait()
    total = l2[0]
    for k in range(1, m):
        total = total + l2[k]
    for q in range(reps):
        line = jnp.zeros((part, LANES), jnp.float32)
        for k in range(per):
            line = jnp.where(grp == k, turn(total[k], (k - q) * width, 1), line)
        lo_ref[q * part : (q + 1) * part, :] = line[:, : per * width]
    for copy in query_sent:
        copy.wait()
    put_stream(0)
    for copy in taps_sent:
        copy.wait()
    for h in range(tiles):
        for r in range(reps):
            line = jnp.zeros((16, LANES), jnp.float32)
            for g in range(reps):
                moved = turn(tgr[h * reps + g], (g - r) * width, 1)
                line = jnp.where(lane_group(16, width) == g, moved, line)
            at = (r * tiles + h) * LANES
            for p in range(streams):
                to_ref[p, :, at : at + LANES] = line[tap_count * p : tap_count * (p + 1)]


def whole_specs(count):
    return [pl.BlockSpec(memory_space=pltpu.VMEM)] * count


def half_tables(tokens):
    step = 32
    col = np.arange(tokens)
    coarse = np.arange(tokens // step)[:, None] * step * col[None, :] % (2 * tokens)
    fine = np.arange(step)[:, None] * col[None, :] % (2 * tokens)
    out = []
    for index in (coarse, fine):
        phase = index * (math.pi / tokens)
        out += [np.cos(phase).astype(np.float32), np.sin(phase).astype(np.float32)]
    return out


def fast_shards(n, m, proj_in, taps, long_filter, out_grad):
    streams, rows, channels = proj_in.shape
    groups = long_filter.shape[1]
    reps = channels // groups
    part = rows // reps
    tokens = n * rows
    f32, bf16 = jnp.float32, jnp.bfloat16
    shape, vmem = jax.ShapeDtypeStruct, pltpu.VMEM
    wide = vmem((tokens, 2 * LANES), bf16)
    full = vmem((tokens, 2 * LANES), f32)
    packs = vmem((n, part, LANES), f32)
    moved = vmem((2, n, 2, rows, LANES), bf16)
    grads = vmem((streams, n, rows, LANES), bf16)
    return pl.pallas_call(
        functools.partial(whole_kernel, n, m, reps),
        out_shape=(
            shape((streams, rows, channels), bf16), shape((rows, groups // m), f32), shape(taps.shape, f32),
        ),
        in_specs=whole_specs(8),
        out_specs=whole_specs(3),
        scratch_shapes=[moved, moved, packs, packs]
        + [vmem((tokens, tokens), bf16)] * 4
        + [wide] * 3 + [full] * 2 + [wide] * 6 + [full, vmem((tokens, LANES), f32)]
        + [grads, grads, packs, packs, vmem((m, n // m, part, LANES), f32)]
        + [vmem((16, LANES), f32), vmem((n, 16, LANES), f32)]
        + [pltpu.SemaphoreType.DMA((2, 8, n - 1)), pltpu.SemaphoreType.DMA((2, m - 1))],
        compiler_params=pltpu.CompilerParams(
            collective_id=0, has_side_effects=True, vmem_limit_bytes=56 << 20
        ),
    )(proj_in, out_grad, long_filter, taps, *half_tables(tokens))


def fits(n, m, proj_in, taps, long_filter, out_grad):
    streams, rows, channels = proj_in.shape
    groups = long_filter.shape[1]
    if channels % groups or groups % n or n % m or streams != 3 or taps.shape[1] != 3:
        return False
    reps, width = channels // groups, groups // n
    if reps < 2 or reps * width != LANES or n % reps or rows % (8 * reps) or rows % 16:
        return False
    return n * rows <= TABLE_LIMIT and n * rows % 256 == 0


def routed(n, m, *arrays):
    return fast_shards(n, m, *arrays) if fits(n, m, *arrays) else shards(*arrays)


def solution(mesh):
    return jax.shard_map(
        functools.partial(routed, mesh.shape["seq"], mesh.shape["chan"]),
        mesh=mesh,
        in_specs=(P(None, "seq", "chan"), P(None, None, "chan"), P("seq", None), P("seq", "chan")),
        out_specs=(P(None, "seq", "chan"), P("seq", "chan"), P(None, None, "chan")),
        check_vma=False,
    )
```

```python
import functools
import math

import jax
import jax.numpy as jnp
import numpy as np
from jax import lax
from jax.experimental import pallas as pl
from jax.experimental.pallas import tpu as pltpu
from jax.sharding import PartitionSpec as P

MESH = pl.DeviceIdType.MESH
LANES = 128
TABLE_LIMIT = 1024


def shifted(x, axis, by):
    devices = lax.axis_size(axis)
    pairs = [(i, i + by) for i in range(devices) if 0 <= i + by < devices]
    return lax.ppermute(x, axis, pairs)


def angle_table(left_index, right_index, period):
    product = left_index[:, None] * right_index[None, :] % period
    phase = product.astype(jnp.float32) * (2.0 * math.pi / period)
    return (jnp.cos(phase), jnp.sin(phase))


def contract(pattern, factor_table, operand):
    return jnp.einsum(pattern, factor_table, operand, precision=lax.Precision.HIGHEST)


def steps_of(count):
    return jnp.arange(count, dtype=jnp.int32)


def whole_forward(signal, seq_width):
    tok_rows, stack_count, channels = signal.shape
    period = 2 * seq_width * tok_rows
    narrow = channels // seq_width
    arrived = lax.all_to_all(signal, "seq", split_axis=2, concat_axis=0, tiled=True)
    laid = arrived.reshape(seq_width, tok_rows, stack_count, narrow).transpose(2, 3, 0, 1)
    cos_step, sin_step = angle_table(steps_of(2 * seq_width), steps_of(seq_width), 2 * seq_width)
    real_part = contract("qm,ncmj->ncqj", cos_step, laid)
    imag_part = -contract("qm,ncmj->ncqj", sin_step, laid)
    cos_turn, sin_turn = angle_table(steps_of(2 * seq_width), steps_of(tok_rows), period)
    turned_re = real_part * cos_turn + imag_part * sin_turn
    turned_im = imag_part * cos_turn - real_part * sin_turn
    cos_row, sin_row = angle_table(steps_of(tok_rows), steps_of(tok_rows), tok_rows)
    spec_re = contract("rj,ncqj->ncqr", cos_row, turned_re) + contract(
        "rj,ncqj->ncqr", sin_row, turned_im
    )
    spec_im = contract("rj,ncqj->ncqr", cos_row, turned_im) - contract(
        "rj,ncqj->ncqr", sin_row, turned_re
    )
    return (spec_re, spec_im)


def whole_inverse(spec_re, spec_im, seq_width):
    stack_count, narrow, freq_count, tok_rows = spec_re.shape
    period = 2 * seq_width * tok_rows
    cos_row, sin_row = angle_table(steps_of(tok_rows), steps_of(tok_rows), tok_rows)
    back_re = contract("rj,ncqr->ncqj", cos_row, spec_re) - contract(
        "rj,ncqr->ncqj", sin_row, spec_im
    )
    back_im = contract("rj,ncqr->ncqj", sin_row, spec_re) + contract(
        "rj,ncqr->ncqj", cos_row, spec_im
    )
    cos_turn, sin_turn = angle_table(steps_of(freq_count), steps_of(tok_rows), period)
    turned_re = back_re * cos_turn - back_im * sin_turn
    turned_im = back_re * sin_turn + back_im * cos_turn
    cos_step, sin_step = angle_table(steps_of(seq_width), steps_of(freq_count), freq_count)
    signal = contract("mq,ncqj->ncmj", cos_step, turned_re) - contract(
        "mq,ncqj->ncmj", sin_step, turned_im
    )
    signal = (
        (signal / period).transpose(2, 3, 0, 1).reshape(seq_width * tok_rows, stack_count, narrow)
    )
    return lax.all_to_all(signal, "seq", split_axis=0, concat_axis=2, tiled=True)


def member(values, index, stack_axis):
    return lax.index_in_dim(values, index, stack_axis, keepdims=False)


def shards(proj_in, taps, long_filter, out_grad):
    stream_count, tok_rows, channels = proj_in.shape
    tap_count = taps.shape[1]
    groups = long_filter.shape[1]
    seq_width = lax.axis_size("seq")
    lower_rim = shifted(proj_in[:, tok_rows - (tap_count - 1) :, :], "seq", 1)
    extended = jnp.concatenate([lower_rim, proj_in], axis=1).astype(jnp.float32)
    lagged = [
        extended[:, tap_count - 1 - lag_step : tap_count - 1 - lag_step + tok_rows, :]
        for lag_step in range(tap_count)
    ]
    featured = taps[:, 0, None, :] * lagged[0]
    for lag_step in range(1, tap_count):
        featured = featured + taps[:, lag_step, None, :] * lagged[lag_step]
    query_rows, key_rows, value_rows = (featured[0], featured[1], featured[2])
    mixed_rows = key_rows * value_rows
    upstream = out_grad.astype(jnp.float32)
    conv_grad = upstream * query_rows
    tiled_filter = jnp.tile(long_filter, (1, channels // groups))
    signals = jnp.stack([mixed_rows, conv_grad, tiled_filter], axis=1)
    data_re, data_im = whole_forward(signals, seq_width)
    stack_axis = 0
    mix_re, mix_im = (member(data_re, 0, stack_axis), member(data_im, 0, stack_axis))
    grad_re, grad_im = (member(data_re, 1, stack_axis), member(data_im, 1, stack_axis))
    filt_re, filt_im = (member(data_re, 2, stack_axis), member(data_im, 2, stack_axis))
    conv_re = filt_re * mix_re - filt_im * mix_im
    conv_im = filt_re * mix_im + filt_im * mix_re
    back_re = filt_re * grad_re + filt_im * grad_im
    back_im = filt_re * grad_im - filt_im * grad_re
    corr_re = grad_re * mix_re + grad_im * mix_im
    corr_im = grad_im * mix_re - grad_re * mix_im
    prod_re = jnp.stack([conv_re, back_re, corr_re], axis=stack_axis)
    prod_im = jnp.stack([conv_im, back_im, corr_im], axis=stack_axis)
    outputs = whole_inverse(prod_re, prod_im, seq_width)
    conv_out, mixed_grad = (outputs[:, 0], outputs[:, 1])
    filt_grad = jnp.sum(outputs[:, 2].reshape(tok_rows, channels // groups, groups), axis=1)
    long_grad = lax.psum_scatter(filt_grad, "chan", scatter_dimension=1, tiled=True)
    feature_grad = jnp.stack(
        [upstream * conv_out, mixed_grad * value_rows, mixed_grad * key_rows], axis=0
    )
    upper_rim = shifted(feature_grad[:, : tap_count - 1, :], "seq", -1)
    trailing = jnp.concatenate([feature_grad, upper_rim], axis=1)
    input_grad = taps[:, 0, None, :] * feature_grad
    for lag_step in range(1, tap_count):
        input_grad = (
            input_grad + taps[:, lag_step, None, :] * trailing[:, lag_step : lag_step + tok_rows]
        )
    partial_taps = jnp.stack(
        [jnp.sum(feature_grad * lagged[lag_step], axis=1) for lag_step in range(tap_count)], axis=1
    )
    tap_grad = lax.psum(partial_taps, "seq") / math.sqrt(seq_width * tok_rows)
    return (input_grad.astype(jnp.bfloat16), long_grad, tap_grad)


def meet(axis_sizes):
    barrier = pltpu.get_barrier_semaphore()
    total = 0
    for axis, size in axis_sizes:
        me = lax.axis_index(axis)
        for j in range(1, size):
            pl.semaphore_signal(
                barrier, inc=1, device_id={axis: lax.rem(me + j, size)}, device_id_type=MESH
            )
        total += size - 1
    pl.semaphore_wait(barrier, total)


def swap_matrix(reps, width):
    side = reps * LANES
    row = lax.broadcasted_iota(jnp.int32, (side, side), 0)
    col = lax.broadcasted_iota(jnp.int32, (side, side), 1)
    outer, inner, rest = row // LANES, (row % LANES) // width, row % width
    hit = inner * LANES + outer * width + rest == col
    return jnp.where(hit, 1.0, 0.0).astype(jnp.bfloat16)


def lane_group(rows, width):
    return lax.broadcasted_iota(jnp.int32, (rows, LANES), 1) // width


def turn(x, shift, axis):
    shift = shift % x.shape[axis]
    return x if shift == 0 else pltpu.roll(x, shift, axis)


def halves(x):
    high = x.astype(jnp.bfloat16)
    return high, (x - high.astype(jnp.float32)).astype(jnp.bfloat16)


def later(x, lag):
    if lag == 0:
        return x
    row = lax.broadcasted_iota(jnp.int32, x.shape, 0)
    return jnp.where(row < lag, 0.0, pltpu.roll(x, lag, 0))


def sooner(x, lag):
    if lag == 0:
        return x
    row = lax.broadcasted_iota(jnp.int32, x.shape, 0)
    return jnp.where(row >= x.shape[0] - lag, 0.0, pltpu.roll(x, x.shape[0] - lag, 0))


def group_sum(x, reps):
    total = x
    for r in range(1, reps):
        total = total + turn(x, r * (LANES // reps), 1)
    return total


def three(high, low, x_high, x_low):
    def dot(a, b):
        return jnp.dot(a, b, preferred_element_type=jnp.float32)

    return dot(high, x_high) + (dot(high, x_low) + dot(low, x_high))


def make_table(ca, sa, cb, sb, ch, cl, sh, sl):
    step = cb.shape[0]

    @pl.loop(0, ca.shape[0])
    def _(i):
        c0, s0 = ca[pl.ds(i, 1), :], sa[pl.ds(i, 1), :]
        rows = pl.ds(pl.multiple_of(i * step, step), step)
        ch[rows, :], cl[rows, :] = halves(c0 * cb[...] - s0 * sb[...])
        sh[rows, :], sl[rows, :] = halves(s0 * cb[...] + c0 * sb[...])


def whole_kernel(
    n, m, reps, x_ref, og_ref, lf_ref, tp_ref, ca, sa, cb, sb, out_ref, lo_ref, to_ref,
    xs, xr, fs, fr, ch, cl, sh, sl, mh, ml, gg, sa_f, sb_f, eh, el, oh, ol, ec, oc, res, res0,
    igs, igr, lgs, lgc, lsum, lgr, l2, tgs, tgr, sems, csems,
):
    me, mine = lax.axis_index("seq"), lax.axis_index("chan")
    width = LANES // reps
    streams, rows, _ = x_ref.shape
    tap_count = tp_ref.shape[1]
    tokens = n * rows
    part = rows // reps
    share = part // m
    tiles = n // reps
    meet([("seq", n), ("chan", m)])
    grp = lane_group(part, width)

    def ship(kind, source, target):
        copies = []
        for j in range(1, n):
            peer = lax.rem(me + j, n)
            copy = pltpu.make_async_remote_copy(
                src_ref=source(peer), dst_ref=target, send_sem=sems.at[0, kind, j - 1],
                recv_sem=sems.at[1, kind, j - 1], device_id={"seq": peer}, device_id_type=MESH,
            )
            copy.start()
            copies.append(copy)
        return copies

    def spread(kind, source, target):
        copies = []
        for j in range(1, m):
            peer = lax.rem(mine + j, m)
            copy = pltpu.make_async_remote_copy(
                src_ref=source(peer), dst_ref=target, send_sem=csems.at[0, kind, j - 1],
                recv_sem=csems.at[1, kind, j - 1], device_id={"chan": peer}, device_id_type=MESH,
            )
            copy.start()
            copies.append(copy)
        return copies

    swap = swap_matrix(reps, width)

    def gather_stream(source, place):
        for h in range(tiles):
            joined = jnp.concatenate(
                [source[:, (r * tiles + h) * LANES : (r * tiles + h + 1) * LANES] for r in range(reps)],
                axis=1,
            )
            moved = jnp.dot(joined, swap, preferred_element_type=jnp.float32).astype(jnp.bfloat16)
            for g in range(reps):
                xs[place // 2, h * reps + g, place % 2] = moved[:, g * LANES : (g + 1) * LANES]

    for s in range(n):
        base = (s // reps) * LANES
        packed = jnp.zeros((part, LANES), jnp.float32)
        for q in range(reps):
            tile = lf_ref[q * part : (q + 1) * part, base : base + LANES]
            packed = jnp.where(grp == q, turn(tile, (q - s % reps) * width, 1), packed)
        fs[s] = packed.reshape(m, share, LANES)
    filter_sent = ship(1, lambda peer: fs.at[peer, mine], fr.at[mine, me])
    gather_stream(x_ref.at[0], 0)
    gather_stream(og_ref, 1)
    first = ship(0, lambda peer: xs.at[0, peer], xr.at[0, me])
    gather_stream(x_ref.at[1], 2)
    gather_stream(x_ref.at[2], 3)
    second = ship(2, lambda peer: xs.at[1, peer], xr.at[1, me])
    xr[0, me] = xs[0, me]
    xr[1, me] = xs[1, me]
    fr[mine, me] = fs[me, mine]

    taps = []
    home, slot = me // reps, lax.rem(me, reps)
    for p in range(streams):
        mixed_taps = jnp.zeros((tap_count, LANES), jnp.float32)
        for r in range(reps):
            at = pl.multiple_of((r * tiles + home) * LANES, LANES)
            tile = tp_ref[p, :, pl.ds(at, LANES)]
            shift = lax.rem((r + reps - slot) * width, LANES)
            mixed_taps = jnp.where(
                lane_group(tap_count, width) == r, pltpu.roll(tile, shift, 1), mixed_taps
            )
        taps.append([mixed_taps[i : i + 1] for i in range(tap_count)])
    tgs[...] = jnp.zeros_like(tgs)
    make_table(ca, sa, cb, sb, ch, cl, sh, sl)

    for copy in filter_sent:
        copy.wait()
    filter_passed = spread(0, lambda peer: fr.at[mine], fr.at[mine])

    places = {0: (0, 0), 3: (0, 1), 1: (1, 0), 2: (1, 1)}

    def stream(p):
        half, at = places[p]
        return xr[half, :, at].reshape(tokens, LANES).astype(jnp.float32)

    def feature(p):
        x = stream(p)
        total = taps[p][0] * x
        for lag in range(1, tap_count):
            total = total + taps[p][lag] * later(x, lag)
        return total

    def alternating(count):
        row = lax.broadcasted_iota(jnp.int32, (count, LANES), 0)
        return jnp.where(row % 2 == 0, 1.0, -1.0)

    def dot(left, right):
        return jnp.dot(left, right, preferred_element_type=jnp.float32)

    def paired(high, low, both):
        wide = dot(high, both[...])
        return wide[:, :LANES] + (wide[:, LANES:] + dot(low, both[:, :LANES]))

    def weight_of(i, count):
        row = lax.broadcasted_iota(jnp.int32, (count, LANES), 0) + i * count
        return jnp.where(row == 0, 0.5 / tokens, 1.0 / tokens)

    for copy in first:
        copy.wait()
    sign = alternating(tokens)
    grad = stream(3) * feature(0)
    mh[:, :LANES], ml[:, :LANES] = halves(grad)
    grad_end = jnp.sum(sign * grad, axis=0, keepdims=True)
    filt_end = jnp.zeros((1, LANES), jnp.float32)
    for copy in filter_passed:
        copy.wait()
    for s in range(n):
        packed = jnp.concatenate([fr[k, s] for k in range(m)], axis=0)
        for q in range(reps):
            piece = group_sum(jnp.where(grp == q, packed, 0.0), reps)
            filt_end = filt_end + jnp.sum(alternating(part) * piece, axis=0, keepdims=True)
            at = s * rows + q * part
            mh[at : at + part, LANES:], ml[at : at + part, LANES:] = halves(piece)
    chunk = min(256, tokens)

    @pl.loop(0, tokens // chunk)
    def _(i):
        at = pl.ds(pl.multiple_of(i * chunk, chunk), chunk)
        a = three(ch[at, :], cl[at, :], mh[...], ml[...])
        b = three(sh[at, :], sl[at, :], mh[...], ml[...])
        sa_f[at, :], sb_f[at, :] = a, b
        ag, af, bg, bf = a[:, :LANES], a[:, LANES:], b[:, :LANES], b[:, LANES:]
        weight = weight_of(i, chunk)
        ec[at, :LANES], ec[at, LANES:] = halves((af * ag + bf * bg) * weight)
        oc[at, :LANES], oc[at, LANES:] = halves((af * bg - bf * ag) * weight)

    back_end = filt_end * grad_end * (0.5 / tokens)

    @pl.loop(0, tokens // chunk)
    def _(i):
        at = pl.ds(pl.multiple_of(i * chunk, chunk), chunk)
        total = paired(ch[at, :], cl[at, :], ec) + paired(sh[at, :], sl[at, :], oc)
        row = lax.broadcasted_iota(jnp.int32, total.shape, 0)
        res0[at, :] = total + jnp.where(row % 2 == 0, back_end, -back_end)

    for copy in second:
        copy.wait()

    def finish(p, grads, place):
        total = taps[p][0] * grads
        for lag in range(1, tap_count):
            total = total + taps[p][lag] * sooner(grads, lag)
        place[...] = total.astype(jnp.bfloat16).reshape(n, rows, LANES)

    def tap_lines(p, grads):
        x = stream(p)
        for lag in range(tap_count):
            line = jnp.sum(grads * later(x, lag), axis=0, keepdims=True)
            tgs[tap_count * p + lag : tap_count * p + lag + 1, :] = line * (1.0 / math.sqrt(tokens))

    key_rows, value_rows = feature(1), feature(2)
    mixed = key_rows * value_rows
    gg[:, :LANES], gg[:, LANES:] = halves(mixed)
    mixed_end = jnp.sum(sign * mixed, axis=0, keepdims=True)
    finish(1, res0[...] * value_rows, igs.at[1])
    key_sent = ship(4, lambda peer: igs.at[1, peer], igr.at[1, me])
    finish(2, res0[...] * key_rows, igs.at[2])
    value_sent = ship(5, lambda peer: igs.at[2, peer], igr.at[2, me])

    @pl.loop(0, tokens // chunk)
    def _(i):
        at = pl.ds(pl.multiple_of(i * chunk, chunk), chunk)
        am = paired(ch[at, :], cl[at, :], gg)
        bm = paired(sh[at, :], sl[at, :], gg)
        ag, af, bg, bf = sa_f[at, :LANES], sa_f[at, LANES:], sb_f[at, :LANES], sb_f[at, LANES:]
        weight = weight_of(i, chunk)
        eh[at, :LANES], el[at, :LANES] = halves((af * am - bf * bm) * weight)
        oh[at, :LANES], ol[at, :LANES] = halves((af * bm + bf * am) * weight)
        eh[at, LANES:], el[at, LANES:] = halves(group_sum(ag * am + bg * bm, reps) * weight)
        oh[at, LANES:], ol[at, LANES:] = halves(group_sum(bg * am - ag * bm, reps) * weight)

    ends = jnp.concatenate(
        [filt_end * mixed_end, group_sum(grad_end * mixed_end, reps)], axis=1
    ) * (0.5 / tokens)

    @pl.loop(0, tokens // chunk)
    def _(i):
        at = pl.ds(pl.multiple_of(i * chunk, chunk), chunk)
        total = three(ch[at, :], cl[at, :], eh[...], el[...])
        total = total + three(sh[at, :], sl[at, :], oh[...], ol[...])
        row = lax.broadcasted_iota(jnp.int32, total.shape, 0)
        res[at, :] = total + jnp.where(row % 2 == 0, ends, -ends)

    for s in range(n):
        packed = jnp.zeros((part, LANES), jnp.float32)
        for q in range(reps):
            at = s * rows + q * part
            packed = jnp.where(grp == q, res[at : at + part, LANES:], packed)
        for k in range(m):
            lgs[k, s] = packed[k * share : (k + 1) * share]
    long_parts = spread(1, lambda peer: lgs.at[peer], lgc.at[mine])
    lgc[mine] = lgs[mine]
    query_grads = stream(3) * res[:, :LANES]
    finish(0, query_grads, igs.at[0])
    for copy in long_parts:
        copy.wait()
    summed = lgc[0]
    for k in range(1, m):
        summed = summed + lgc[k]
    lsum[...] = summed
    long_sent = ship(3, lambda peer: lsum.at[peer], lgr.at[me])
    lgr[me] = lsum[me]
    query_sent = ship(6, lambda peer: igs.at[0, peer], igr.at[0, me])
    tap_lines(0, query_grads)
    tap_lines(1, res0[...] * feature(2))
    tap_lines(2, res0[...] * feature(1))
    taps_sent = ship(7, lambda peer: tgs, tgr.at[me])
    tgr[me] = tgs[...]
    for p in range(streams):
        igr[p, me] = igs[p, me]
    for copy in long_sent:
        copy.wait()
    per = n // m
    chan_sent = spread(2, lambda peer: lgr.at[pl.ds(peer * per, per)], l2.at[mine])
    l2[mine] = lgr[pl.ds(mine * per, per)]

    def put_stream(p):
        for h in range(tiles):
            joined = jnp.concatenate([igr[p, h * reps + g] for g in range(reps)], axis=1)
            moved = dot(joined, swap).astype(jnp.bfloat16)
            for r in range(reps):
                at = (r * tiles + h) * LANES
                out_ref[p, :, at : at + LANES] = moved[:, r * LANES : (r + 1) * LANES]

    for copy in key_sent:
        copy.wait()
    put_stream(1)
    for copy in value_sent:
        copy.wait()
    put_stream(2)
    for copy in chan_sent:
        copy.wait()
    sources = [jnp.concatenate([l2[q, k] for q in range(m)], axis=0) for k in range(per)]
    lines = []
    for q in range(reps):
        line = jnp.zeros((part, LANES), jnp.float32)
        for k in range(per):
            line = jnp.where(grp == k, turn(sources[k], (k - q) * width, 1), line)
        lines.append(line)
    lo_ref[...] = jnp.concatenate(lines, axis=0).T[: per * width]
    for copy in query_sent:
        copy.wait()
    put_stream(0)
    for copy in taps_sent:
        copy.wait()
    for h in range(tiles):
        for r in range(reps):
            line = jnp.zeros((16, LANES), jnp.float32)
            for g in range(reps):
                moved = turn(tgr[h * reps + g], (g - r) * width, 1)
                line = jnp.where(lane_group(16, width) == g, moved, line)
            at = (r * tiles + h) * LANES
            for p in range(streams):
                to_ref[p, :, at : at + LANES] = line[tap_count * p : tap_count * (p + 1)]


def whole_specs(count):
    return [pl.BlockSpec(memory_space=pltpu.VMEM)] * count


def half_tables(tokens):
    step = 32
    col = np.arange(tokens)
    coarse = np.arange(tokens // step)[:, None] * step * col[None, :] % (2 * tokens)
    fine = np.arange(step)[:, None] * col[None, :] % (2 * tokens)
    out = []
    for index in (coarse, fine):
        phase = index * (math.pi / tokens)
        out += [np.cos(phase).astype(np.float32), np.sin(phase).astype(np.float32)]
    return out


def fast_shards(n, m, proj_in, taps, long_filter, out_grad):
    streams, rows, channels = proj_in.shape
    groups = long_filter.shape[1]
    reps = channels // groups
    part = rows // reps
    tokens = n * rows
    f32, bf16 = jnp.float32, jnp.bfloat16
    shape, vmem = jax.ShapeDtypeStruct, pltpu.VMEM
    wide = vmem((tokens, 2 * LANES), bf16)
    full = vmem((tokens, 2 * LANES), f32)
    share = part // m
    quarters = vmem((m, n, share, LANES), f32)
    quarter = vmem((n, share, LANES), f32)
    moved = vmem((2, n, 2, rows, LANES), bf16)
    grads = vmem((streams, n, rows, LANES), bf16)
    out, long_grad, tap_grad = pl.pallas_call(
        functools.partial(whole_kernel, n, m, reps),
        out_shape=(
            shape((streams, rows, channels), bf16), shape((groups // m, rows), f32), shape(taps.shape, f32),
        ),
        in_specs=whole_specs(8),
        out_specs=whole_specs(3),
        scratch_shapes=[moved, moved, vmem((n, m, share, LANES), f32), quarters]
        + [vmem((tokens, tokens), bf16)] * 4
        + [wide] * 3 + [full] * 2 + [wide] * 6 + [full, vmem((tokens, LANES), f32)]
        + [grads, grads, quarters, quarters, quarter, quarter, vmem((m, n // m, share, LANES), f32)]
        + [vmem((16, LANES), f32), vmem((n, 16, LANES), f32)]
        + [pltpu.SemaphoreType.DMA((2, 8, n - 1)), pltpu.SemaphoreType.DMA((2, 3, m - 1))],
        compiler_params=pltpu.CompilerParams(
            collective_id=0, has_side_effects=True, vmem_limit_bytes=56 << 20
        ),
    )(proj_in, out_grad, long_filter, taps, *half_tables(tokens))
    return (out, long_grad.T, tap_grad)


def fits(n, m, proj_in, taps, long_filter, out_grad):
    streams, rows, channels = proj_in.shape
    groups = long_filter.shape[1]
    if channels % groups or groups % n or n % m or streams != 3 or taps.shape[1] != 3:
        return False
    reps, width = channels // groups, groups // n
    if reps < 2 or reps * width != LANES or n % reps or rows % (8 * reps * m) or rows % LANES:
        return False
    return n * rows <= TABLE_LIMIT and n * rows % 256 == 0


def routed(n, m, *arrays):
    return fast_shards(n, m, *arrays) if fits(n, m, *arrays) else shards(*arrays)


def solution(mesh):
    return jax.shard_map(
        functools.partial(routed, mesh.shape["seq"], mesh.shape["chan"]),
        mesh=mesh,
        in_specs=(P(None, "seq", "chan"), P(None, None, "chan"), P("seq", None), P("seq", "chan")),
        out_specs=(P(None, "seq", "chan"), P("seq", "chan"), P(None, None, "chan")),
        check_vma=False,
    )
```

```python
import functools
import math

import jax
import jax.numpy as jnp
import numpy as np
from jax import lax
from jax.experimental import pallas as pl
from jax.experimental.pallas import tpu as pltpu
from jax.sharding import PartitionSpec as P

MESH = pl.DeviceIdType.MESH
LANES = 128
TABLE_LIMIT = 1024


def shifted(x, axis, by):
    devices = lax.axis_size(axis)
    pairs = [(i, i + by) for i in range(devices) if 0 <= i + by < devices]
    return lax.ppermute(x, axis, pairs)


def angle_table(left_index, right_index, period):
    product = left_index[:, None] * right_index[None, :] % period
    phase = product.astype(jnp.float32) * (2.0 * math.pi / period)
    return (jnp.cos(phase), jnp.sin(phase))


def contract(pattern, factor_table, operand):
    return jnp.einsum(pattern, factor_table, operand, precision=lax.Precision.HIGHEST)


def steps_of(count):
    return jnp.arange(count, dtype=jnp.int32)


def whole_forward(signal, seq_width):
    tok_rows, stack_count, channels = signal.shape
    period = 2 * seq_width * tok_rows
    narrow = channels // seq_width
    arrived = lax.all_to_all(signal, "seq", split_axis=2, concat_axis=0, tiled=True)
    laid = arrived.reshape(seq_width, tok_rows, stack_count, narrow).transpose(2, 3, 0, 1)
    cos_step, sin_step = angle_table(steps_of(2 * seq_width), steps_of(seq_width), 2 * seq_width)
    real_part = contract("qm,ncmj->ncqj", cos_step, laid)
    imag_part = -contract("qm,ncmj->ncqj", sin_step, laid)
    cos_turn, sin_turn = angle_table(steps_of(2 * seq_width), steps_of(tok_rows), period)
    turned_re = real_part * cos_turn + imag_part * sin_turn
    turned_im = imag_part * cos_turn - real_part * sin_turn
    cos_row, sin_row = angle_table(steps_of(tok_rows), steps_of(tok_rows), tok_rows)
    spec_re = contract("rj,ncqj->ncqr", cos_row, turned_re) + contract(
        "rj,ncqj->ncqr", sin_row, turned_im
    )
    spec_im = contract("rj,ncqj->ncqr", cos_row, turned_im) - contract(
        "rj,ncqj->ncqr", sin_row, turned_re
    )
    return (spec_re, spec_im)


def whole_inverse(spec_re, spec_im, seq_width):
    stack_count, narrow, freq_count, tok_rows = spec_re.shape
    period = 2 * seq_width * tok_rows
    cos_row, sin_row = angle_table(steps_of(tok_rows), steps_of(tok_rows), tok_rows)
    back_re = contract("rj,ncqr->ncqj", cos_row, spec_re) - contract(
        "rj,ncqr->ncqj", sin_row, spec_im
    )
    back_im = contract("rj,ncqr->ncqj", sin_row, spec_re) + contract(
        "rj,ncqr->ncqj", cos_row, spec_im
    )
    cos_turn, sin_turn = angle_table(steps_of(freq_count), steps_of(tok_rows), period)
    turned_re = back_re * cos_turn - back_im * sin_turn
    turned_im = back_re * sin_turn + back_im * cos_turn
    cos_step, sin_step = angle_table(steps_of(seq_width), steps_of(freq_count), freq_count)
    signal = contract("mq,ncqj->ncmj", cos_step, turned_re) - contract(
        "mq,ncqj->ncmj", sin_step, turned_im
    )
    signal = (
        (signal / period).transpose(2, 3, 0, 1).reshape(seq_width * tok_rows, stack_count, narrow)
    )
    return lax.all_to_all(signal, "seq", split_axis=0, concat_axis=2, tiled=True)


def member(values, index, stack_axis):
    return lax.index_in_dim(values, index, stack_axis, keepdims=False)


def shards(proj_in, taps, long_filter, out_grad):
    stream_count, tok_rows, channels = proj_in.shape
    tap_count = taps.shape[1]
    groups = long_filter.shape[1]
    seq_width = lax.axis_size("seq")
    lower_rim = shifted(proj_in[:, tok_rows - (tap_count - 1) :, :], "seq", 1)
    extended = jnp.concatenate([lower_rim, proj_in], axis=1).astype(jnp.float32)
    lagged = [
        extended[:, tap_count - 1 - lag_step : tap_count - 1 - lag_step + tok_rows, :]
        for lag_step in range(tap_count)
    ]
    featured = taps[:, 0, None, :] * lagged[0]
    for lag_step in range(1, tap_count):
        featured = featured + taps[:, lag_step, None, :] * lagged[lag_step]
    query_rows, key_rows, value_rows = (featured[0], featured[1], featured[2])
    mixed_rows = key_rows * value_rows
    upstream = out_grad.astype(jnp.float32)
    conv_grad = upstream * query_rows
    tiled_filter = jnp.tile(long_filter, (1, channels // groups))
    signals = jnp.stack([mixed_rows, conv_grad, tiled_filter], axis=1)
    data_re, data_im = whole_forward(signals, seq_width)
    stack_axis = 0
    mix_re, mix_im = (member(data_re, 0, stack_axis), member(data_im, 0, stack_axis))
    grad_re, grad_im = (member(data_re, 1, stack_axis), member(data_im, 1, stack_axis))
    filt_re, filt_im = (member(data_re, 2, stack_axis), member(data_im, 2, stack_axis))
    conv_re = filt_re * mix_re - filt_im * mix_im
    conv_im = filt_re * mix_im + filt_im * mix_re
    back_re = filt_re * grad_re + filt_im * grad_im
    back_im = filt_re * grad_im - filt_im * grad_re
    corr_re = grad_re * mix_re + grad_im * mix_im
    corr_im = grad_im * mix_re - grad_re * mix_im
    prod_re = jnp.stack([conv_re, back_re, corr_re], axis=stack_axis)
    prod_im = jnp.stack([conv_im, back_im, corr_im], axis=stack_axis)
    outputs = whole_inverse(prod_re, prod_im, seq_width)
    conv_out, mixed_grad = (outputs[:, 0], outputs[:, 1])
    filt_grad = jnp.sum(outputs[:, 2].reshape(tok_rows, channels // groups, groups), axis=1)
    long_grad = lax.psum_scatter(filt_grad, "chan", scatter_dimension=1, tiled=True)
    feature_grad = jnp.stack(
        [upstream * conv_out, mixed_grad * value_rows, mixed_grad * key_rows], axis=0
    )
    upper_rim = shifted(feature_grad[:, : tap_count - 1, :], "seq", -1)
    trailing = jnp.concatenate([feature_grad, upper_rim], axis=1)
    input_grad = taps[:, 0, None, :] * feature_grad
    for lag_step in range(1, tap_count):
        input_grad = (
            input_grad + taps[:, lag_step, None, :] * trailing[:, lag_step : lag_step + tok_rows]
        )
    partial_taps = jnp.stack(
        [jnp.sum(feature_grad * lagged[lag_step], axis=1) for lag_step in range(tap_count)], axis=1
    )
    tap_grad = lax.psum(partial_taps, "seq") / math.sqrt(seq_width * tok_rows)
    return (input_grad.astype(jnp.bfloat16), long_grad, tap_grad)


def meet(axis_sizes):
    barrier = pltpu.get_barrier_semaphore()
    total = 0
    for axis, size in axis_sizes:
        me = lax.axis_index(axis)
        for j in range(1, size):
            pl.semaphore_signal(
                barrier, inc=1, device_id={axis: lax.rem(me + j, size)}, device_id_type=MESH
            )
        total += size - 1
    pl.semaphore_wait(barrier, total)


def swap_matrix(reps, width):
    side = reps * LANES
    row = lax.broadcasted_iota(jnp.int32, (side, side), 0)
    col = lax.broadcasted_iota(jnp.int32, (side, side), 1)
    outer, inner, rest = row // LANES, (row % LANES) // width, row % width
    hit = inner * LANES + outer * width + rest == col
    return jnp.where(hit, 1.0, 0.0).astype(jnp.bfloat16)


def lane_group(rows, width):
    return lax.broadcasted_iota(jnp.int32, (rows, LANES), 1) // width


def turn(x, shift, axis):
    shift = shift % x.shape[axis]
    return x if shift == 0 else pltpu.roll(x, shift, axis)


def halves(x):
    high = x.astype(jnp.bfloat16)
    return high, (x - high.astype(jnp.float32)).astype(jnp.bfloat16)


def later(x, lag):
    if lag == 0:
        return x
    row = lax.broadcasted_iota(jnp.int32, x.shape, 0)
    return jnp.where(row < lag, 0.0, pltpu.roll(x, lag, 0))


def sooner(x, lag):
    if lag == 0:
        return x
    row = lax.broadcasted_iota(jnp.int32, x.shape, 0)
    return jnp.where(row >= x.shape[0] - lag, 0.0, pltpu.roll(x, x.shape[0] - lag, 0))


def group_sum(x, reps):
    total = x
    for r in range(1, reps):
        total = total + turn(x, r * (LANES // reps), 1)
    return total


def three(high, low, x_high, x_low):
    def dot(a, b):
        return jnp.dot(a, b, preferred_element_type=jnp.float32)

    return dot(high, x_high) + (dot(high, x_low) + dot(low, x_high))


def make_table(ca, sa, cb, sb, ch, cl, sh, sl):
    step = cb.shape[0]

    @pl.loop(0, ca.shape[0])
    def _(i):
        c0, s0 = ca[pl.ds(i, 1), :], sa[pl.ds(i, 1), :]
        rows = pl.ds(pl.multiple_of(i * step, step), step)
        ch[rows, :], cl[rows, :] = halves(c0 * cb[...] - s0 * sb[...])
        sh[rows, :], sl[rows, :] = halves(s0 * cb[...] + c0 * sb[...])


def whole_kernel(
    n, m, reps, x_ref, og_ref, lf_ref, tp_ref, ca, sa, cb, sb, out_ref, lo_ref, to_ref,
    xs, xr, fs, fr, ch, cl, sh, sl, mh, ml, gg, sa_f, sb_f, eh, el, oh, ol, ec, oc, res, res0,
    igs, igr, lgs, lgc, lsum, lgr, l2, tgs, tgr, sems, csems,
):
    me, mine = lax.axis_index("seq"), lax.axis_index("chan")
    width = LANES // reps
    streams, rows, _ = x_ref.shape
    tap_count = tp_ref.shape[1]
    tokens = n * rows
    part = rows // reps
    share = part // m
    tiles = n // reps
    meet([("seq", n), ("chan", m)])
    grp = lane_group(part, width)

    def ship(kind, source, target):
        copies = []
        for j in sorted(range(1, n), key=lambda j: abs(2 * j - n)):
            peer = lax.rem(me + j, n)
            copy = pltpu.make_async_remote_copy(
                src_ref=source(peer), dst_ref=target, send_sem=sems.at[0, kind, j - 1],
                recv_sem=sems.at[1, kind, j - 1], device_id={"seq": peer}, device_id_type=MESH,
            )
            copy.start()
            copies.append(copy)
        return copies

    def spread(kind, source, target):
        copies = []
        for j in range(1, m):
            peer = lax.rem(mine + j, m)
            copy = pltpu.make_async_remote_copy(
                src_ref=source(peer), dst_ref=target, send_sem=csems.at[0, kind, j - 1],
                recv_sem=csems.at[1, kind, j - 1], device_id={"chan": peer}, device_id_type=MESH,
            )
            copy.start()
            copies.append(copy)
        return copies

    swap = swap_matrix(reps, width)

    def gather_stream(source, place):
        for h in range(tiles):
            joined = jnp.concatenate(
                [source[:, (r * tiles + h) * LANES : (r * tiles + h + 1) * LANES] for r in range(reps)],
                axis=1,
            )
            moved = jnp.dot(joined, swap, preferred_element_type=jnp.float32).astype(jnp.bfloat16)
            for g in range(reps):
                xs[place // 2, h * reps + g, place % 2] = moved[:, g * LANES : (g + 1) * LANES]

    for s in range(n):
        base = (s // reps) * LANES
        packed = jnp.zeros((part, LANES), jnp.float32)
        for q in range(reps):
            tile = lf_ref[q * part : (q + 1) * part, base : base + LANES]
            packed = jnp.where(grp == q, turn(tile, (q - s % reps) * width, 1), packed)
        fs[s] = packed.reshape(m, share, LANES)
    filter_sent = ship(1, lambda peer: fs.at[peer, mine], fr.at[mine, me])
    gather_stream(x_ref.at[0], 0)
    gather_stream(og_ref, 1)
    first = ship(0, lambda peer: xs.at[0, peer], xr.at[0, me])
    gather_stream(x_ref.at[1], 2)
    gather_stream(x_ref.at[2], 3)
    second = ship(2, lambda peer: xs.at[1, peer], xr.at[1, me])
    xr[0, me] = xs[0, me]
    xr[1, me] = xs[1, me]
    fr[mine, me] = fs[me, mine]

    taps = []
    home, slot = me // reps, lax.rem(me, reps)
    for p in range(streams):
        mixed_taps = jnp.zeros((tap_count, LANES), jnp.float32)
        for r in range(reps):
            at = pl.multiple_of((r * tiles + home) * LANES, LANES)
            tile = tp_ref[p, :, pl.ds(at, LANES)]
            shift = lax.rem((r + reps - slot) * width, LANES)
            mixed_taps = jnp.where(
                lane_group(tap_count, width) == r, pltpu.roll(tile, shift, 1), mixed_taps
            )
        taps.append([mixed_taps[i : i + 1] for i in range(tap_count)])
    tgs[...] = jnp.zeros_like(tgs)
    make_table(ca, sa, cb, sb, ch, cl, sh, sl)

    for copy in filter_sent:
        copy.wait()
    filter_passed = spread(0, lambda peer: fr.at[mine], fr.at[mine])

    places = {0: (0, 0), 3: (0, 1), 1: (1, 0), 2: (1, 1)}

    def stream(p):
        half, at = places[p]
        return xr[half, :, at].reshape(tokens, LANES).astype(jnp.float32)

    def feature(p):
        x = stream(p)
        total = taps[p][0] * x
        for lag in range(1, tap_count):
            total = total + taps[p][lag] * later(x, lag)
        return total

    def alternating(count):
        row = lax.broadcasted_iota(jnp.int32, (count, LANES), 0)
        return jnp.where(row % 2 == 0, 1.0, -1.0)

    def dot(left, right):
        return jnp.dot(left, right, preferred_element_type=jnp.float32)

    def paired(high, low, both):
        wide = dot(high, both[...])
        return wide[:, :LANES] + (wide[:, LANES:] + dot(low, both[:, :LANES]))

    def weight_of(i, count):
        row = lax.broadcasted_iota(jnp.int32, (count, LANES), 0) + i * count
        return jnp.where(row == 0, 0.5 / tokens, 1.0 / tokens)

    for copy in first:
        copy.wait()
    sign = alternating(tokens)
    grad = stream(3) * feature(0)
    mh[:, :LANES], ml[:, :LANES] = halves(grad)
    grad_end = jnp.sum(sign * grad, axis=0, keepdims=True)
    filt_end = jnp.zeros((1, LANES), jnp.float32)
    for copy in filter_passed:
        copy.wait()
    for s in range(n):
        packed = jnp.concatenate([fr[k, s] for k in range(m)], axis=0)
        for q in range(reps):
            piece = group_sum(jnp.where(grp == q, packed, 0.0), reps)
            filt_end = filt_end + jnp.sum(alternating(part) * piece, axis=0, keepdims=True)
            at = s * rows + q * part
            mh[at : at + part, LANES:], ml[at : at + part, LANES:] = halves(piece)
    chunk = min(256, tokens)

    @pl.loop(0, tokens // chunk)
    def _(i):
        at = pl.ds(pl.multiple_of(i * chunk, chunk), chunk)
        a = three(ch[at, :], cl[at, :], mh[...], ml[...])
        b = three(sh[at, :], sl[at, :], mh[...], ml[...])
        sa_f[at, :], sb_f[at, :] = a, b
        ag, af, bg, bf = a[:, :LANES], a[:, LANES:], b[:, :LANES], b[:, LANES:]
        weight = weight_of(i, chunk)
        ec[at, :LANES], ec[at, LANES:] = halves((af * ag + bf * bg) * weight)
        oc[at, :LANES], oc[at, LANES:] = halves((af * bg - bf * ag) * weight)

    back_end = filt_end * grad_end * (0.5 / tokens)

    @pl.loop(0, tokens // chunk)
    def _(i):
        at = pl.ds(pl.multiple_of(i * chunk, chunk), chunk)
        total = paired(ch[at, :], cl[at, :], ec) + paired(sh[at, :], sl[at, :], oc)
        row = lax.broadcasted_iota(jnp.int32, total.shape, 0)
        res0[at, :] = total + jnp.where(row % 2 == 0, back_end, -back_end)

    for copy in second:
        copy.wait()

    def finish(p, grads, place):
        total = taps[p][0] * grads
        for lag in range(1, tap_count):
            total = total + taps[p][lag] * sooner(grads, lag)
        place[...] = total.astype(jnp.bfloat16).reshape(n, rows, LANES)

    def tap_lines(p, grads):
        x = stream(p)
        for lag in range(tap_count):
            line = jnp.sum(grads * later(x, lag), axis=0, keepdims=True)
            tgs[tap_count * p + lag : tap_count * p + lag + 1, :] = line * (1.0 / math.sqrt(tokens))

    key_rows, value_rows = feature(1), feature(2)
    mixed = key_rows * value_rows
    gg[:, :LANES], gg[:, LANES:] = halves(mixed)
    mixed_end = jnp.sum(sign * mixed, axis=0, keepdims=True)
    finish(1, res0[...] * value_rows, igs.at[1])
    key_sent = ship(4, lambda peer: igs.at[1, peer], igr.at[1, me])
    finish(2, res0[...] * key_rows, igs.at[2])
    value_sent = ship(5, lambda peer: igs.at[2, peer], igr.at[2, me])

    @pl.loop(0, tokens // chunk)
    def _(i):
        at = pl.ds(pl.multiple_of(i * chunk, chunk), chunk)
        am = paired(ch[at, :], cl[at, :], gg)
        bm = paired(sh[at, :], sl[at, :], gg)
        ag, af, bg, bf = sa_f[at, :LANES], sa_f[at, LANES:], sb_f[at, :LANES], sb_f[at, LANES:]
        weight = weight_of(i, chunk)
        eh[at, :LANES], el[at, :LANES] = halves((af * am - bf * bm) * weight)
        oh[at, :LANES], ol[at, :LANES] = halves((af * bm + bf * am) * weight)
        eh[at, LANES:], el[at, LANES:] = halves(group_sum(ag * am + bg * bm, reps) * weight)
        oh[at, LANES:], ol[at, LANES:] = halves(group_sum(bg * am - ag * bm, reps) * weight)

    ends = jnp.concatenate(
        [filt_end * mixed_end, group_sum(grad_end * mixed_end, reps)], axis=1
    ) * (0.5 / tokens)

    @pl.loop(0, tokens // chunk)
    def _(i):
        at = pl.ds(pl.multiple_of(i * chunk, chunk), chunk)
        total = three(ch[at, :], cl[at, :], eh[...], el[...])
        total = total + three(sh[at, :], sl[at, :], oh[...], ol[...])
        row = lax.broadcasted_iota(jnp.int32, total.shape, 0)
        res[at, :] = total + jnp.where(row % 2 == 0, ends, -ends)

    for s in range(n):
        packed = jnp.zeros((part, LANES), jnp.float32)
        for q in range(reps):
            at = s * rows + q * part
            packed = jnp.where(grp == q, res[at : at + part, LANES:], packed)
        for k in range(m):
            lgs[k, s] = packed[k * share : (k + 1) * share]
    long_parts = spread(1, lambda peer: lgs.at[peer], lgc.at[mine])
    lgc[mine] = lgs[mine]
    query_grads = stream(3) * res[:, :LANES]
    finish(0, query_grads, igs.at[0])
    for copy in long_parts:
        copy.wait()
    summed = lgc[0]
    for k in range(1, m):
        summed = summed + lgc[k]
    lsum[...] = summed
    long_sent = ship(3, lambda peer: lsum.at[peer], lgr.at[me])
    lgr[me] = lsum[me]
    query_sent = ship(6, lambda peer: igs.at[0, peer], igr.at[0, me])
    tap_lines(0, query_grads)
    tap_lines(1, res0[...] * feature(2))
    tap_lines(2, res0[...] * feature(1))
    taps_sent = ship(7, lambda peer: tgs, tgr.at[me])
    tgr[me] = tgs[...]
    for p in range(streams):
        igr[p, me] = igs[p, me]
    for copy in long_sent:
        copy.wait()
    per = n // m
    chan_sent = spread(2, lambda peer: lgr.at[pl.ds(peer * per, per)], l2.at[mine])
    l2[mine] = lgr[pl.ds(mine * per, per)]

    def put_stream(p):
        for h in range(tiles):
            joined = jnp.concatenate([igr[p, h * reps + g] for g in range(reps)], axis=1)
            moved = dot(joined, swap).astype(jnp.bfloat16)
            for r in range(reps):
                at = (r * tiles + h) * LANES
                out_ref[p, :, at : at + LANES] = moved[:, r * LANES : (r + 1) * LANES]

    for copy in key_sent:
        copy.wait()
    put_stream(1)
    for copy in value_sent:
        copy.wait()
    put_stream(2)
    for copy in chan_sent:
        copy.wait()
    sources = [jnp.concatenate([l2[q, k] for q in range(m)], axis=0) for k in range(per)]
    lines = []
    for q in range(reps):
        line = jnp.zeros((part, LANES), jnp.float32)
        for k in range(per):
            line = jnp.where(grp == k, turn(sources[k], (k - q) * width, 1), line)
        lines.append(line)
    lo_ref[...] = jnp.concatenate(lines, axis=0).T[: per * width]
    for copy in query_sent:
        copy.wait()
    put_stream(0)
    for copy in taps_sent:
        copy.wait()
    for h in range(tiles):
        for r in range(reps):
            line = jnp.zeros((16, LANES), jnp.float32)
            for g in range(reps):
                moved = turn(tgr[h * reps + g], (g - r) * width, 1)
                line = jnp.where(lane_group(16, width) == g, moved, line)
            at = (r * tiles + h) * LANES
            for p in range(streams):
                to_ref[p, :, at : at + LANES] = line[tap_count * p : tap_count * (p + 1)]


def whole_specs(count):
    return [pl.BlockSpec(memory_space=pltpu.VMEM)] * count


def half_tables(tokens):
    step = 32
    col = np.arange(tokens)
    coarse = np.arange(tokens // step)[:, None] * step * col[None, :] % (2 * tokens)
    fine = np.arange(step)[:, None] * col[None, :] % (2 * tokens)
    out = []
    for index in (coarse, fine):
        phase = index * (math.pi / tokens)
        out += [np.cos(phase).astype(np.float32), np.sin(phase).astype(np.float32)]
    return out


def fast_shards(n, m, proj_in, taps, long_filter, out_grad):
    streams, rows, channels = proj_in.shape
    groups = long_filter.shape[1]
    reps = channels // groups
    part = rows // reps
    tokens = n * rows
    f32, bf16 = jnp.float32, jnp.bfloat16
    shape, vmem = jax.ShapeDtypeStruct, pltpu.VMEM
    wide = vmem((tokens, 2 * LANES), bf16)
    full = vmem((tokens, 2 * LANES), f32)
    share = part // m
    quarters = vmem((m, n, share, LANES), f32)
    quarter = vmem((n, share, LANES), f32)
    moved = vmem((2, n, 2, rows, LANES), bf16)
    grads = vmem((streams, n, rows, LANES), bf16)
    out, long_grad, tap_grad = pl.pallas_call(
        functools.partial(whole_kernel, n, m, reps),
        out_shape=(
            shape((streams, rows, channels), bf16), shape((groups // m, rows), f32), shape(taps.shape, f32),
        ),
        in_specs=whole_specs(8),
        out_specs=whole_specs(3),
        scratch_shapes=[moved, moved, vmem((n, m, share, LANES), f32), quarters]
        + [vmem((tokens, tokens), bf16)] * 4
        + [wide] * 3 + [full] * 2 + [wide] * 6 + [full, vmem((tokens, LANES), f32)]
        + [grads, grads, quarters, quarters, quarter, quarter, vmem((m, n // m, share, LANES), f32)]
        + [vmem((16, LANES), f32), vmem((n, 16, LANES), f32)]
        + [pltpu.SemaphoreType.DMA((2, 8, n - 1)), pltpu.SemaphoreType.DMA((2, 3, m - 1))],
        compiler_params=pltpu.CompilerParams(
            collective_id=0, has_side_effects=True, vmem_limit_bytes=56 << 20
        ),
    )(proj_in, out_grad, long_filter, taps, *half_tables(tokens))
    return (out, long_grad.T, tap_grad)


def fits(n, m, proj_in, taps, long_filter, out_grad):
    streams, rows, channels = proj_in.shape
    groups = long_filter.shape[1]
    if channels % groups or groups % n or n % m or streams != 3 or taps.shape[1] != 3:
        return False
    reps, width = channels // groups, groups // n
    if reps < 2 or reps * width != LANES or n % reps or rows % (8 * reps * m) or rows % LANES:
        return False
    return n * rows <= TABLE_LIMIT and n * rows % 256 == 0


def routed(n, m, *arrays):
    return fast_shards(n, m, *arrays) if fits(n, m, *arrays) else shards(*arrays)


def solution(mesh):
    return jax.shard_map(
        functools.partial(routed, mesh.shape["seq"], mesh.shape["chan"]),
        mesh=mesh,
        in_specs=(P(None, "seq", "chan"), P(None, None, "chan"), P("seq", None), P("seq", "chan")),
        out_specs=(P(None, "seq", "chan"), P("seq", "chan"), P(None, None, "chan")),
        check_vma=False,
    )
```
